256 devices in a mesh: dp: 32 (over x, z_hi, core), expert: 8 (over y, z_lo).
Axes of the slice: x: 4, y: 4, z: 8 (z_hi: 4, z_lo: 2; z = z_hi * 2 + z_lo), core: 2. Of those that a mesh axis runs over, the one named last changes fastest.
Arguments:
- tokens: bfloat16 [73728, 2048], P(('dp', 'expert')), may hold values from -24 to 24
- expert_ids: int32 [73728, 8], P(('dp', 'expert')), may hold values from 0 to 127, all different within a row
- gates: float32 [73728, 8], P(('dp', 'expert')), may hold values from 0.05 to 1
- cotangent: bfloat16 [73728, 2048], P(('dp', 'expert')), may hold values from -1.25 to 1.25
- gate_weight: bfloat16 [8, 2048, 768], P('expert'), may hold values from -0.125 to 0.125
- up_weight: bfloat16 [8, 2048, 768], P('expert'), may hold values from -0.125 to 0.125
- down_weight: bfloat16 [8, 2048, 768], P('expert'), may hold values from -0.21875 to 0.21875
- block_masks: int32 [8, 3, 16, 6], P('expert'), may hold values 0 or 1
Outputs:
- combined: bfloat16 [73728, 2048], P(('dp', 'expert'))
- grad_gate: float32 [8, 2048, 768], P('expert', 'dp')
- grad_up: float32 [8, 2048, 768], P('expert', 'dp')
- grad_down: float32 [8, 2048, 768], P('expert', 'dp')
The draws below stay inside these ranges and needn't reach their ends.
Inputs may be any that keep to these rules, and one draw needn't show every extreme that they name: `expert_ids`: each row names 8 different experts.
All inputs are finite; a program needn't handle non-finite values. No bound on the sum of `block_masks` on one device may be relied on, other than what follows from the above.
Results may differ from the reference program's by a relative error of at most 0.014.
Values may be sent and summed in bfloat16 or wider, within the bound.
A program may use at most 128 MiB of HBM per device.

```python
import math
import jax
import jax.numpy as jnp
from jax import lax

D = 2048
FF = 768
ALL_EXPERTS = 128
TOP = 8
TILE = 128
MICRO = 2
TOK_MB = 144
EXPERTS = 8
CAP = 18
TOKENS = 73728
N_DP = 32
N_EXPERT = 8


def touch_ends(drawn, stream_key, least, top_value):
    place = [jax.random.randint(jax.random.fold_in(stream_key, axis), (), 0, length) for axis, length in enumerate(drawn.shape)]
    main_axis = drawn.shape.index(max(drawn.shape))
    beside = place[:main_axis] + [(place[main_axis] + 1) % drawn.shape[main_axis]] + place[main_axis + 1:]
    return drawn.at[tuple(place)].set(least).at[tuple(beside)].set(top_value)


def strengthened(array, rng, source, target, blocks, factor):
    owner, partner = [(jnp.arange(array.shape[position]) // (array.shape[position] // blocks)).reshape([-1 if axis == position else 1 for axis in range(array.ndim)]) for position in (source, target)]
    chosen = jax.random.permutation(rng, blocks)[partner]
    strong = (owner == chosen) | (owner == (partner + blocks // 2) % blocks)
    return jnp.where(strong, factor * array, array)


def block_levels(own_key, extent, cuts, low, high):
    def one(dim, blocks):
        draws = jax.random.uniform(jax.random.fold_in(jax.random.fold_in(own_key, 6), dim), (blocks,), jnp.float32, low / len(cuts), high / len(cuts))
        return jnp.repeat(jnp.exp(draws), extent[dim] // blocks).reshape((-1,) + (1,) * (len(extent) - dim - 1))

    factor_of = one(*cuts[0])
    for cut in cuts[1:]:
        factor_of = factor_of * one(*cut)
    return factor_of


def distinct(key, rows, number_of, top, lift):
    ranking = jax.random.permutation(jax.random.fold_in(key, 1), number_of)
    boost = ranking
    for power in range(3):
        boost = boost * boost // number_of
    boost = boost * lift // number_of
    tickets = jax.random.randint(jax.random.fold_in(key, 2), (rows, number_of), 0, 4096) + boost
    holders = jax.random.permutation(jax.random.fold_in(key, 3), rows)[jnp.arange(number_of) % rows]
    tickets = jnp.where(jnp.arange(rows)[:, None] == holders[None, :], 1 << 14, tickets)
    priority = tickets * number_of + jnp.arange(number_of)
    return lax.top_k(priority.astype(jnp.int32), top)[1].astype(jnp.int32)


def scatter_about(own_key, extent, deviation, bound, shards=(), held_as=jnp.bfloat16):
    factor_of = block_levels(own_key, extent, shards, -0.22, 0.18) if shards else 1.0
    entries = jax.random.normal(own_key, extent, jnp.float32) * deviation * factor_of
    return jnp.minimum(jnp.maximum(entries, -bound), bound).astype(held_as)


def bell_draw_with(own_key, dims, deviation, most, pieces, heavy, held_as=jnp.bfloat16):
    drawn = deviation * jax.random.normal(own_key, dims, jnp.float32)
    if pieces:
        drawn = drawn * block_levels(own_key, dims, pieces, -0.22, 0.18)
    return jnp.clip(strengthened(drawn, jax.random.fold_in(own_key, 3), *heavy), -most, most).astype(held_as)


def setup_inputs(seed: int = 0) -> dict:
    streams_of = jax.random.split(jax.random.key(seed), 9)
    tokens = bell_draw_with(streams_of[0], (TOKENS, D), 1.0, 24.0, ((0, 256),), (0, 1, 256, 6.0))
    expert_ids = distinct(streams_of[1], TOKENS, ALL_EXPERTS, TOP, 512)
    gates = jnp.clip(jnp.exp(math.log(1.0) - 2.9957323 * jax.random.uniform(streams_of[2], (TOKENS, TOP), jnp.float32) ** block_levels(streams_of[2], (TOKENS, TOP), ((0, 256),), -0.2, 0.2)), 0.05, 1.0)
    cotangent = bell_draw_with(streams_of[3], (TOKENS, D), 0.05, 1.25, ((0, 256),), (0, 1, 256, 6.0))
    gate_weight = scatter_about(streams_of[4], (EXPERTS, D, FF), D ** -0.5, 0.125, ((0, 8),))
    up_weight = scatter_about(streams_of[5], (EXPERTS, D, FF), D ** -0.5, 0.125, ((0, 8),))
    down_weight = scatter_about(streams_of[6], (EXPERTS, D, FF), FF ** -0.5, 0.21875, ((0, 8),))
    block_masks = touch_ends((jax.random.randint(streams_of[7], (EXPERTS, 3, D // TILE, FF // TILE), 0, 5) < 2).astype(jnp.int32), jax.random.fold_in(streams_of[7], 1), 0, 1)
    return dict(tokens=tokens, expert_ids=expert_ids, gates=gates, cotangent=cotangent, gate_weight=gate_weight, up_weight=up_weight, down_weight=down_weight, block_masks=block_masks)


def expand_masks(block_masks):
    count, three, row_blocks, col_blocks = block_masks.shape
    spread = jnp.broadcast_to(block_masks.astype(jnp.bfloat16)[:, :, :, None, :, None], (count, three, row_blocks, TILE, col_blocks, TILE))
    return spread.reshape(count, three, row_blocks * TILE, col_blocks * TILE)


def route(ids, gates):
    onehot = (ids[:, :, None] == jnp.arange(EXPERTS, dtype=jnp.int32)).astype(jnp.int32)
    flat = onehot.reshape(-1, EXPERTS)
    before = jnp.cumsum(flat, axis=0) - flat
    slot_index = jnp.sum(before * flat, axis=1)
    which = jnp.sum(flat * jnp.arange(EXPERTS, dtype=jnp.int32), axis=1)
    live = (jnp.sum(flat, axis=1) > 0) & (slot_index < CAP)
    where_to = jnp.where(live, which * CAP + slot_index, -1).reshape(ids.shape)
    select = where_to[:, :, None] == jnp.arange(EXPERTS * CAP, dtype=jnp.int32)
    sends = jnp.sum(select.astype(jnp.float32), axis=1)
    rounded = gates.astype(jnp.bfloat16).astype(jnp.float32)
    weights = jnp.sum(jnp.where(select, rounded[:, :, None], 0.0), axis=1)
    return sends, weights


def reference(tokens, expert_ids, gates, cotangent, gate_weight, up_weight, down_weight, block_masks):
    masks = expand_masks(block_masks)
    mask_f = masks.astype(jnp.float32)
    w_gate = (gate_weight * masks[:, 0]).astype(jnp.float32)
    w_up = (up_weight * masks[:, 1]).astype(jnp.float32)
    w_down = (down_weight * masks[:, 2]).astype(jnp.float32)
    rows = N_EXPERT * CAP
    x_all = tokens.reshape(N_DP, N_EXPERT, MICRO, TOK_MB, D)
    ids_all = expert_ids.reshape(N_DP, N_EXPERT, MICRO, TOK_MB, TOP)
    gates_all = gates.reshape(N_DP, N_EXPERT, MICRO, TOK_MB, TOP)
    dy_all = cotangent.reshape(N_DP, N_EXPERT, MICRO, TOK_MB, D)

    def to_rows(buffer):
        shaped = buffer.reshape(N_EXPERT, MICRO, EXPERTS, CAP, D).transpose(2, 1, 0, 3, 4)
        return shaped.reshape(EXPERTS, MICRO, rows, D)

    def replica(totals, block):
        x_rep, ids_rep, gates_rep, dy_rep = block
        sends, weights = jax.vmap(jax.vmap(route))(ids_rep, gates_rep)
        x_buf = jnp.einsum("smtc,smtd->smcd", sends, x_rep.astype(jnp.float32)).astype(jnp.bfloat16)
        dy_buf = jnp.einsum("smtc,smtd->smcd", weights, dy_rep.astype(jnp.float32)).astype(jnp.bfloat16)
        x_rows = to_rows(x_buf).astype(jnp.float32)
        dy_rows = to_rows(dy_buf).astype(jnp.float32)
        gate_pre = jnp.einsum("emrd,edf->emrf", x_rows, w_gate)
        up_pre = jnp.einsum("emrd,edf->emrf", x_rows, w_up)
        hidden = (jax.nn.silu(gate_pre) * up_pre).astype(jnp.bfloat16)
        result = jnp.einsum("emrf,edf->emrd", hidden.astype(jnp.float32), w_down).astype(jnp.bfloat16)
        back = result.reshape(EXPERTS, MICRO, N_EXPERT, CAP, D).transpose(2, 1, 0, 3, 4)
        back = back.reshape(N_EXPERT, MICRO, EXPERTS * CAP, D)
        combined = jnp.einsum("smtc,smcd->smtd", weights, back.astype(jnp.float32)).astype(jnp.bfloat16)
        d_hidden = jnp.einsum("emrd,edf->emrf", dy_rows, w_down)
        sig = jax.nn.sigmoid(gate_pre)
        d_gate = (d_hidden * up_pre * sig * (1.0 + gate_pre * (1.0 - sig))).astype(jnp.bfloat16)
        d_up = (d_hidden * gate_pre * sig).astype(jnp.bfloat16)
        part_gate = jnp.einsum("emrd,emrf->edf", x_rows, d_gate.astype(jnp.float32)) * mask_f[:, 0]
        part_up = jnp.einsum("emrd,emrf->edf", x_rows, d_up.astype(jnp.float32)) * mask_f[:, 1]
        part_down = jnp.einsum("emrd,emrf->edf", dy_rows, hidden.astype(jnp.float32)) * mask_f[:, 2]
        parts = (part_gate, part_up, part_down)
        new_totals = tuple(total + lax.optimization_barrier(part.astype(jnp.bfloat16)).astype(jnp.float32) for total, part in zip(totals, parts))
        return new_totals, combined

    empty = jnp.zeros((EXPERTS, D, FF), jnp.float32)
    totals, outputs = lax.scan(replica, (empty, empty, empty), (x_all, ids_all, gates_all, dy_all))
    combined = outputs.reshape(N_DP * N_EXPERT * MICRO * TOK_MB, D)
    return (combined, totals[0], totals[1], totals[2])
```

```python
import functools

import jax
import jax.numpy as jnp
from jax import lax
from jax.experimental import pallas as pl
from jax.experimental.pallas import tpu as pltpu
from jax.sharding import PartitionSpec as P

MESH = pl.DeviceIdType.MESH
BF = jnp.bfloat16
F32 = jnp.float32
CAP = 18
E = 8
T = 288
TM = 144
D = 2048
FF = 768
BLK = 128
NB = 18
ROWS = 16
BUCKETS = (12, 13, 14, 18)


def nn(a, b):
    return jnp.dot(a, b, preferred_element_type=F32)


def nt(a, b):
    return lax.dot_general(a, b, (((1,), (1,)), ((), ())), preferred_element_type=F32)


def iota(shape, dim):
    return lax.broadcasted_iota(jnp.int32, shape, dim)


def flag(cond):
    return jnp.where(cond, 1.0, 0.0).astype(BF)


def act_kernel(
    tok_h, ids_ref, gat_ref, cot_h, wg_h, wu_h, wd_h, msk_ref,
    xt_h, yt_h, act_h, rm_h, rr_h, wt_h, tbl_ref, cnt_ref,
    tok, cot, wg, wu, wd, sel, wsel, xs, xsr, ys, ysr, xr, xrr, yr, yrr,
    rem, g, u, acts, rm, rr, xt, yt, wt, mx, cbuf, crec,
    lsem, osem, ssem, rsem,
):
    dp = lax.axis_index("dp")
    me = lax.axis_index("expert")

    loads = [
        pltpu.make_async_copy(tok_h, tok, lsem.at[0]),
        pltpu.make_async_copy(cot_h, cot, lsem.at[1]),
        pltpu.make_async_copy(wg_h, wg, lsem.at[2]),
        pltpu.make_async_copy(wu_h, wu, lsem.at[3]),
        pltpu.make_async_copy(wd_h, wd, lsem.at[4]),
    ]
    for load in loads:
        load.start()

    barrier = pltpu.get_barrier_semaphore()
    for k in range(1, E):
        pl.semaphore_signal(
            barrier, inc=1, device_id=(dp, lax.rem(me + k, E)), device_id_type=MESH
        )

    eye8 = flag(iota((E, E), 0) == iota((E, E), 1))
    ids_t = nt(eye8, ids_ref[...].astype(F32).astype(BF))
    gat_t = nt(eye8, gat_ref[...].astype(BF))
    sub = iota((E, T), 0)
    hit = jnp.zeros((E, T), F32)
    gw = jnp.zeros((E, T), F32)
    for e in range(E):
        same = ids_t == float(e)
        hit = jnp.where(
            sub == e, jnp.sum(jnp.where(same, 1.0, 0.0), axis=0, keepdims=True), hit
        )
        gw = jnp.where(
            sub == e, jnp.sum(jnp.where(same, gat_t, 0.0), axis=0, keepdims=True), gw
        )
    t0 = iota((T, T), 0)
    t1 = iota((T, T), 1)
    earlier = flag((t0 < t1) & ((t0 < TM) == (t1 < TM)))
    before = nn(hit.astype(BF), earlier)
    lane = iota((E, T), 1)
    kept = (hit > 0.0) & (before < float(CAP))
    slot = jnp.where(kept, before + jnp.where(lane < TM, 0.0, float(CAP)), -1.0)
    row8 = iota((T, E), 0)
    owner = jnp.where(row8 < 256, row8 // 32, (row8 - 256) // 4)
    spread = flag(owner == iota((T, E), 1))
    slot_rows = nn(spread, slot.astype(BF))
    gw_rows = nn(spread, gw.astype(BF))
    want = jnp.where(t0 < 256, t0 % 32, 32 + (t0 - 256) % 4).astype(F32)
    chosen = slot_rows == want
    sel[...] = flag(chosen)
    wsel[...] = jnp.where(chosen, gw_rows, 0.0).astype(BF)

    def dispatch(matrix, source, main, tail):
        def step(n, carry):
            cols = pl.ds(pl.multiple_of(n * 512, 512), 512)
            v = nn(matrix[...], source[:, cols])
            main[:, cols] = v[:256].astype(BF)
            for e in range(E):
                tail[e, :, cols] = v[256 + 4 * e : 260 + 4 * e].astype(BF)
            return carry

        lax.fori_loop(0, 4, step, 0)

    def moves(main, tail, main_to, tail_to, kind):
        out = []
        for k in range(1, E):
            to = lax.rem(me + k, E)
            out.append(
                pltpu.make_async_remote_copy(
                    src_ref=main.at[pl.ds(pl.multiple_of(to * 32, 32), 32)],
                    dst_ref=main_to.at[pl.ds(pl.multiple_of(me * 32, 32), 32)],
                    send_sem=ssem.at[kind, k],
                    recv_sem=rsem.at[kind, k],
                    device_id=(dp, to),
                    device_id_type=MESH,
                )
            )
            out.append(
                pltpu.make_async_remote_copy(
                    src_ref=tail.at[to],
                    dst_ref=tail_to.at[me],
                    send_sem=ssem.at[kind + 1, k],
                    recv_sem=rsem.at[kind + 1, k],
                    device_id=(dp, to),
                    device_id_type=MESH,
                )
            )
        own = [
            pltpu.make_async_copy(
                main.at[pl.ds(pl.multiple_of(me * 32, 32), 32)],
                main_to.at[pl.ds(pl.multiple_of(me * 32, 32), 32)],
                lsem.at[5 + kind],
            ),
            pltpu.make_async_copy(tail.at[me], tail_to.at[me], lsem.at[6 + kind]),
        ]
        return out, own

    def merge(main_to, tail_to):
        for e in range(E):
            rem[4 * e : 4 * e + 4, :] = tail_to[e].astype(F32)
        main_to[256:288, :] = rem[...].astype(BF)

    loads[0].wait()
    dispatch(sel, tok, xs, xsr)
    pl.semaphore_wait(barrier, E - 1)
    x_moves, x_own = moves(xs, xsr, xr, xrr, 0)
    for move in x_moves + x_own:
        move.start()
    loads[1].wait()
    dispatch(wsel, cot, ys, ysr)
    y_moves, y_own = moves(ys, ysr, yr, yrr, 2)
    for move in y_moves + y_own:
        move.start()

    widths = (ROWS, BLK)
    m2 = jnp.zeros(widths, F32)
    for mat in range(3):
        put = flag(iota((6, BLK), 1) == iota((6, BLK), 0) + 6 * mat)
        m2 = m2 + nn(msk_ref[mat].astype(F32).astype(BF), put)
    tri = flag(iota((BLK, BLK), 0) <= iota((BLK, BLK), 1))
    upto = nn(m2.astype(BF), tri)
    pos = upto - 1.0
    most = jnp.max(jnp.max(upto, axis=1, keepdims=True), axis=0, keepdims=True)
    cbuf[...] = jnp.broadcast_to(most, (8, BLK))
    order = jnp.zeros(widths, F32)
    cell = iota(widths, 1).astype(F32)
    for i in range(NB):
        here = (pos[:, i : i + 1] == cell) & (m2[:, i : i + 1] > 0.0)
        order = order + jnp.where(here, float(i), 0.0)
    tbl_ref[0:16, :] = order.astype(jnp.int32)
    tbl_ref[16:32, :] = jnp.maximum(pos, 0.0).astype(jnp.int32)
    tbl_ref[32:48, :] = m2.astype(jnp.int32)
    c_moves = []
    for k in range(1, E):
        to = lax.rem(me + k, E)
        c_moves.append(
            pltpu.make_async_remote_copy(
                src_ref=cbuf,
                dst_ref=crec.at[k],
                send_sem=ssem.at[4, k],
                recv_sem=rsem.at[4, k],
                device_id=(dp, to),
                device_id_type=MESH,
            )
        )
    for move in c_moves:
        move.start()

    lift = flag(iota((6, FF), 1) // BLK == iota((6, FF), 0))
    for mat in range(3):
        mx[16 * mat : 16 * mat + 16, :] = nn(msk_ref[mat].astype(F32).astype(BF), lift)
    for load in loads[2:]:
        load.wait()

    def prune(r, carry):
        rows = pl.ds(pl.multiple_of(r * BLK, BLK), BLK)
        for mat, w in enumerate((wg, wu, wd)):
            w[rows, :] = w[rows, :] * mx[pl.ds(16 * mat + r, 1), :].astype(BF)
        return carry

    lax.fori_loop(0, ROWS, prune, 0)
    eye = flag(iota((T, T), 0) == iota((T, T), 1))
    wt[...] = nt(eye, wsel[...]).astype(BF)

    def turn(source, target):
        def step(r, carry):
            cols = pl.ds(pl.multiple_of(r * BLK, BLK), BLK)
            eye_b = flag(iota((BLK, BLK), 0) == iota((BLK, BLK), 1))
            target[r] = nt(eye_b, source[:, cols]).astype(BF)
            return carry

        lax.fori_loop(0, ROWS, step, 0)

    outs = [
        pltpu.make_async_copy(xt, xt_h, osem.at[0]),
        pltpu.make_async_copy(yt, yt_h, osem.at[1]),
        pltpu.make_async_copy(acts, act_h, osem.at[2]),
        pltpu.make_async_copy(rm, rm_h, osem.at[3]),
        pltpu.make_async_copy(rr, rr_h, osem.at[4]),
        pltpu.make_async_copy(wt, wt_h, osem.at[5]),
    ]
    outs[5].start()

    for move in x_own:
        move.wait()
    for move in x_moves:
        move.wait_recv()
    merge(xr, xrr)

    def forward(n, carry):
        cols = pl.ds(pl.multiple_of(n * 256, 256), 256)
        gv = nn(xr[...], wg[:, cols])
        uv = nn(xr[...], wu[:, cols])
        g[:, cols] = gv
        u[:, cols] = uv
        h_cols = pl.ds(pl.multiple_of(2 * FF + n * 256, 256), 256)
        acts[:, h_cols] = (gv * jax.nn.sigmoid(gv) * uv).astype(BF)
        return carry

    lax.fori_loop(0, 3, forward, 0)

    def project(n, carry):
        cols = pl.ds(pl.multiple_of(n * 256, 256), 256)
        v = nt(acts[:, 2 * FF : 3 * FF], wd[cols, :])
        rm[:, cols] = v[:256].astype(BF)
        for e in range(E):
            rr[e, :, cols] = v[256 + 4 * e : 260 + 4 * e].astype(BF)
        return carry

    lax.fori_loop(0, 8, project, 0)
    outs[3].start()
    outs[4].start()
    turn(xr, xt)
    outs[0].start()

    for move in y_own:
        move.wait()
    for move in y_moves:
        move.wait_recv()
    merge(yr, yrr)

    def backward(n, carry):
        cols = pl.ds(pl.multiple_of(n * 256, 256), 256)
        dh = nn(yr[...], wd[:, cols])
        gv = g[:, cols]
        s = jax.nn.sigmoid(gv)
        ds = dh * s
        acts[:, cols] = (ds * u[:, cols] * (1.0 + gv * (1.0 - s))).astype(BF)
        u_cols = pl.ds(pl.multiple_of(FF + n * 256, 256), 256)
        acts[:, u_cols] = (ds * gv).astype(BF)
        return carry

    lax.fori_loop(0, 3, backward, 0)
    outs[2].start()
    turn(yr, yt)
    outs[1].start()

    for move in c_moves:
        move.wait_recv()
    top = cbuf[...]
    for k in range(1, E):
        top = jnp.maximum(top, crec[k])
    cnt_ref[...] = top
    for move in x_moves + y_moves + c_moves:
        move.wait_send()
    for out in outs:
        out.wait()


def grad_kernel(
    cz,
    xt_h, yt_h, act_h, rm_h, rr_h, wt_h, tbl,
    com_h, gg_ref, gu_ref, gd_ref,
    xt, yt, acts, wt, ret, rer, rem, com, blk,
    cs, cr, sm, ra, rb, fp, fm, zz, za, zb, gp, gm,
    lsem, tsem, ssem, rsem, csem, crsem, xsem, xrsem, zsem, zrsem,
):
    na = cz // 2
    nb = cz - na
    dp = lax.axis_index("dp")
    me = lax.axis_index("expert")
    x = dp // 8
    z = (dp // 2) % 4
    c = dp % 2

    def at(xx, zz_, cc):
        return ((xx * 4 + zz_) * 2 + cc, me)

    twin = at(x, z, 1 - c)
    xp = at((x + 1) % 4, z, c)
    xm = at((x + 3) % 4, z, c)
    zp = at(x, (z + 1) % 4, c)
    zm = at(x, (z + 3) % 4, c)

    def x_of(i):
        return (x + (2, 1, 3, 0)[i]) % 4

    def z_of(t):
        step = jnp.where(t == 0, 2, jnp.where(t == 1, 1, jnp.where(t == 2, 3, 0)))
        return (z + step) % 4

    barrier = pltpu.get_barrier_semaphore()
    for peer in (twin, xp, xm, zp, zm):
        pl.semaphore_signal(barrier, inc=1, device_id=peer, device_id_type=MESH)
    for k in range(1, E):
        pl.semaphore_signal(
            barrier, inc=1, device_id=(dp, lax.rem(me + k, E)), device_id_type=MESH
        )

    loads = [
        pltpu.make_async_copy(act_h, acts, lsem.at[0]),
        pltpu.make_async_copy(wt_h, wt, lsem.at[1]),
        pltpu.make_async_copy(
            rm_h.at[pl.ds(pl.multiple_of(me * 32, 32), 32)],
            ret.at[pl.ds(pl.multiple_of(me * 32, 32), 32)],
            lsem.at[2],
        ),
        pltpu.make_async_copy(rr_h.at[me], rer.at[me], lsem.at[3]),
    ]
    loads[0].start()

    def tile_loads(t, i):
        r = x_of(i) * 4 + z_of(t)
        s = t * 4 + i
        return [
            pltpu.make_async_copy(xt_h.at[r], xt.at[s], tsem.at[0, s]),
            pltpu.make_async_copy(yt_h.at[r], yt.at[s], tsem.at[1, s]),
        ]

    for t in range(4):
        for i in range(4):
            for load in tile_loads(t, i):
                load.start()
    for load in loads[1:]:
        load.start()

    pl.semaphore_wait(barrier, 12)

    r_moves = []
    for k in range(1, E):
        to = lax.rem(me + k, E)
        r_moves.append(
            pltpu.make_async_remote_copy(
                src_ref=rm_h.at[pl.ds(pl.multiple_of(to * 32, 32), 32)],
                dst_ref=ret.at[pl.ds(pl.multiple_of(me * 32, 32), 32)],
                send_sem=ssem.at[0, k],
                recv_sem=rsem.at[0, k],
                device_id=(dp, to),
                device_id_type=MESH,
            )
        )
        r_moves.append(
            pltpu.make_async_remote_copy(
                src_ref=rr_h.at[to],
                dst_ref=rer.at[me],
                send_sem=ssem.at[1, k],
                recv_sem=rsem.at[1, k],
                device_id=(dp, to),
                device_id_type=MESH,
            )
        )
    for move in r_moves:
        move.start()

    def core_move(t, i):
        s = t * 4 + i
        return pltpu.make_async_remote_copy(
            src_ref=cs.at[s], dst_ref=cr.at[s],
            send_sem=csem.at[s], recv_sem=crsem.at[s],
            device_id=twin, device_id_type=MESH,
        )

    def x_move(kind, t):
        src, dst, peer = (
            lambda: (sm.at[4 * t, pl.ds(0, na)], ra.at[t], xp),
            lambda: (sm.at[4 * t, pl.ds(na, nb)], rb.at[t], xm),
            lambda: (sm.at[4 * t + 1, pl.ds(na, nb)], fp.at[t, pl.ds(na, nb)], xp),
            lambda: (sm.at[4 * t + 2, pl.ds(0, na)], fm.at[t, pl.ds(0, na)], xm),
            lambda: (sm.at[4 * t + 1, pl.ds(0, na)], fp.at[t, pl.ds(0, na)], xp),
            lambda: (sm.at[4 * t + 2, pl.ds(na, nb)], fm.at[t, pl.ds(na, nb)], xm),
        )[kind]()
        return pltpu.make_async_remote_copy(
            src_ref=src, dst_ref=dst,
            send_sem=xsem.at[kind, t], recv_sem=xrsem.at[kind, t],
            device_id=peer, device_id_type=MESH,
        )

    def z_move(kind):
        src, dst, peer = (
            lambda: (zz.at[0, pl.ds(0, na)], za, zp),
            lambda: (zz.at[0, pl.ds(na, nb)], zb, zm),
            lambda: (zz.at[1, pl.ds(na, nb)], gp.at[pl.ds(na, nb)], zp),
            lambda: (zz.at[2, pl.ds(0, na)], gm.at[pl.ds(0, na)], zm),
            lambda: (zz.at[1, pl.ds(0, na)], gp.at[pl.ds(0, na)], zp),
            lambda: (zz.at[2, pl.ds(na, nb)], gm.at[pl.ds(na, nb)], zm),
        )[kind]()
        return pltpu.make_async_remote_copy(
            src_ref=src, dst_ref=dst,
            send_sem=zsem.at[kind], recv_sem=zrsem.at[kind],
            device_id=peer, device_id_type=MESH,
        )

    loads[0].wait()

    def wide(v):
        return v.astype(F32)

    def round_trip(t, carry):
        @pl.when(t < 4)
        def _():
            for i in range(4):
                for load in tile_loads(t, i):
                    load.wait()
            tiles = pl.ds(4 * t, 4)

            def tile(n, source):
                cols = pl.ds(pl.multiple_of(n * 256, 256), 256)
                v = nn(source[tiles].reshape(4 * BLK, T), acts[:, cols])
                for i in range(4):
                    for h in range(2):
                        blk[i, 2 * n + h] = v[
                            BLK * i : BLK * i + BLK, BLK * h : BLK * h + BLK
                        ].astype(BF)

            def from_x(n, carry):
                tile(n, xt)
                return carry

            def from_y(n, carry):
                tile(n, yt)
                return carry

            lax.fori_loop(0, 6, from_x, 0)
            lax.fori_loop(6, 9, from_y, 0)
            for i in range(4):
                r = x_of(i) * 4 + z_of(t)
                s = 4 * t + i
                for j in range(cz):
                    b = tbl[r, j]
                    cs[s, j] = blk[i, b, pl.ds(pl.multiple_of(64 * (1 - c), 64), 64), :]
                    sm[s, j] = blk[i, b, pl.ds(pl.multiple_of(64 * c, 64), 64), :]
                core_move(t, i).start()

        @pl.when(t >= 1)
        def _():
            p = t - 1
            x_move(0, p).wait_recv()
            for j in range(na):
                sm[4 * p + 1, j] = (wide(sm[4 * p + 1, j]) + wide(ra[p, j])).astype(BF)
            x_move(4, p).start()
            x_move(1, p).wait_recv()
            for j in range(nb):
                sm[4 * p + 2, na + j] = (
                    wide(sm[4 * p + 2, na + j]) + wide(rb[p, j])
                ).astype(BF)
            x_move(5, p).start()

        @pl.when(t < 4)
        def _():
            for i in range(4):
                s = 4 * t + i
                core_move(t, i).wait_recv()
                for j in range(cz):
                    sm[s, j] = (wide(sm[s, j]) + wide(cr[s, j])).astype(BF)
                if i == 0:
                    x_move(0, t).start()
                    x_move(1, t).start()
                if i == 1:
                    x_move(2, t).start()
                if i == 2:
                    x_move(3, t).start()

        @pl.when((t >= 1) & (t < 4))
        def _():
            p = t - 1
            for kind in (2, 3, 4, 5):
                x_move(kind, p).wait_recv()
            for j in range(cz):
                zz[p, j] = (
                    wide(sm[4 * p + 3, j]) + wide(fp[p, j]) + wide(fm[p, j])
                ).astype(BF)

        @pl.when(t == 1)
        def _():
            z_move(0).start()
            z_move(1).start()

        @pl.when(t == 2)
        def _():
            z_move(2).start()
            z_move(0).wait_recv()
            for j in range(na):
                zz[1, j] = (wide(zz[1, j]) + wide(za[j])).astype(BF)
            z_move(4).start()

        @pl.when(t == 3)
        def _():
            z_move(3).start()
            z_move(1).wait_recv()
            for j in range(nb):
                zz[2, na + j] = (wide(zz[2, na + j]) + wide(zb[j])).astype(BF)
            z_move(5).start()

        return carry

    lax.fori_loop(0, 5, round_trip, 0)

    for load in loads[1:]:
        load.wait()
    for move in r_moves:
        move.wait_recv()
    for e in range(E):
        rem[4 * e : 4 * e + 4, :] = rer[e].astype(F32)
    ret[256:288, :] = rem[...].astype(BF)

    def combine(n, carry):
        cols = pl.ds(pl.multiple_of(n * 512, 512), 512)
        com[:, cols] = nn(wt[...], ret[:, cols]).astype(BF)
        return carry

    lax.fori_loop(0, 4, combine, 0)
    put = pltpu.make_async_copy(com, com_h, lsem.at[4])
    put.start()

    for kind in (2, 3, 4, 5):
        x_move(kind, 3).wait_recv()
        z_move(kind).wait_recv()
    r = x * 4 + z
    for i in range(NB):
        p = tbl[16 + r, i]
        m = tbl[32 + r, i].astype(F32)
        v = wide(sm[15, p]) + wide(fp[3, p]) + wide(fm[3, p]) + wide(gp[p]) + wide(gm[p])
        out = (gg_ref, gu_ref, gd_ref)[i // 6]
        out[:, BLK * (i % 6) : BLK * (i % 6) + BLK] = v * m

    for move in r_moves:
        move.wait_send()

    def drain(t, carry):
        for i in range(4):
            core_move(t, i).wait_send()
        for kind in range(6):
            x_move(kind, t).wait_send()
        return carry

    lax.fori_loop(0, 4, drain, 0)
    for kind in range(6):
        z_move(kind).wait_send()
    put.wait()


def body(tokens, expert_ids, gates, cotangent, gate_weight, up_weight, down_weight, block_masks):
    any_spec = pl.BlockSpec(memory_space=pl.ANY)
    vmem = pl.BlockSpec(memory_space=pltpu.VMEM)
    shape = jax.ShapeDtypeStruct
    dma = pltpu.SemaphoreType.DMA
    xt, yt, acts, rm, rr, wt, tbl, cnt = pl.pallas_call(
        act_kernel,
        out_shape=[
            shape((ROWS, BLK, T), BF),
            shape((ROWS, BLK, T), BF),
            shape((T, 3 * FF), BF),
            shape((256, D), BF),
            shape((E, 4, D), BF),
            shape((T, T), BF),
            shape((48, BLK), jnp.int32),
            shape((8, BLK), F32),
        ],
        in_specs=[any_spec, vmem, vmem] + [any_spec] * 4 + [vmem],
        out_specs=[any_spec] * 6 + [vmem, vmem],
        scratch_shapes=[
            pltpu.VMEM((T, D), BF),
            pltpu.VMEM((T, D), BF),
            pltpu.VMEM((D, FF), BF),
            pltpu.VMEM((D, FF), BF),
            pltpu.VMEM((D, FF), BF),
            pltpu.VMEM((T, T), BF),
            pltpu.VMEM((T, T), BF),
            pltpu.VMEM((256, D), BF),
            pltpu.VMEM((E, 4, D), BF),
            pltpu.VMEM((256, D), BF),
            pltpu.VMEM((E, 4, D), BF),
            pltpu.VMEM((T, D), BF),
            pltpu.VMEM((E, 4, D), BF),
            pltpu.VMEM((T, D), BF),
            pltpu.VMEM((E, 4, D), BF),
            pltpu.VMEM((32, D), F32),
            pltpu.VMEM((T, FF), F32),
            pltpu.VMEM((T, FF), F32),
            pltpu.VMEM((T, 3 * FF), BF),
            pltpu.VMEM((256, D), BF),
            pltpu.VMEM((E, 4, D), BF),
            pltpu.VMEM((ROWS, BLK, T), BF),
            pltpu.VMEM((ROWS, BLK, T), BF),
            pltpu.VMEM((T, T), BF),
            pltpu.VMEM((48, FF), F32),
            pltpu.VMEM((8, BLK), F32),
            pltpu.VMEM((E, 8, BLK), F32),
            dma((9,)),
            dma((6,)),
            dma((5, E)),
            dma((5, E)),
        ],
        compiler_params=pltpu.CompilerParams(collective_id=0, has_side_effects=True),
        name="act",
    )(
        tokens, expert_ids, gates, cotangent,
        gate_weight[0], up_weight[0], down_weight[0], block_masks[0],
    )

    def grads(index, cz):
        na, nb = cz // 2, cz - cz // 2

        def buf(*lead):
            return pltpu.VMEM(lead + (64, BLK), BF)

        return pl.pallas_call(
            functools.partial(grad_kernel, cz),
            out_shape=[
                shape((T, D), BF),
                shape((64, FF), F32),
                shape((64, FF), F32),
                shape((64, FF), F32),
            ],
            in_specs=[any_spec] * 6 + [pl.BlockSpec(memory_space=pltpu.SMEM)],
            out_specs=[any_spec, vmem, vmem, vmem],
            scratch_shapes=[
                pltpu.VMEM((ROWS, BLK, T), BF),
                pltpu.VMEM((ROWS, BLK, T), BF),
                pltpu.VMEM((T, 3 * FF), BF),
                pltpu.VMEM((T, T), BF),
                pltpu.VMEM((T, D), BF),
                pltpu.VMEM((E, 4, D), BF),
                pltpu.VMEM((32, D), F32),
                pltpu.VMEM((T, D), BF),
                pltpu.VMEM((4, NB, BLK, BLK), BF),
                buf(16, cz), buf(16, cz), buf(16, cz),
                buf(4, na), buf(4, nb), buf(4, cz), buf(4, cz),
                buf(3, cz), buf(na), buf(nb), buf(cz), buf(cz),
                dma((5,)),
                dma((2, 16)),
                dma((2, E)),
                dma((2, E)),
                dma((16,)),
                dma((16,)),
                dma((6, 4)),
                dma((6, 4)),
                dma((6,)),
                dma((6,)),
            ],
            compiler_params=pltpu.CompilerParams(
                collective_id=1 + index, has_side_effects=True
            ),
            name=f"grad{cz}",
        )

    most = cnt[0, 0]
    bucket = sum((most > cz).astype(jnp.int32) for cz in BUCKETS[:-1])
    combined, gg, gu, gd = lax.switch(
        bucket,
        [lambda *ops, f=grads(i, cz): tuple(f(*ops)) for i, cz in enumerate(BUCKETS)],
        xt, yt, acts, rm, rr, wt, tbl,
    )
    return (combined, gg[None], gu[None], gd[None])


def solution(mesh):
    return jax.shard_map(
        body,
        mesh=mesh,
        in_specs=(
            P(("dp", "expert"), None),
            P(("dp", "expert"), None),
            P(("dp", "expert"), None),
            P(("dp", "expert"), None),
            P("expert", None, None),
            P("expert", None, None),
            P("expert", None, None),
            P("expert", None, None, None),
        ),
        out_specs=(
            P(("dp", "expert"), None),
            P("expert", "dp", None),
            P("expert", "dp", None),
            P("expert", "dp", None),
        ),
        check_vma=False,
    )
```

```python
import functools

import jax
import jax.numpy as jnp
from jax import lax
from jax.experimental import pallas as pl
from jax.experimental.pallas import tpu as pltpu
from jax.sharding import PartitionSpec as P

MESH = pl.DeviceIdType.MESH
BF = jnp.bfloat16
F32 = jnp.float32
CAP = 18
E = 8
T = 288
TM = 144
D = 2048
FF = 768
BLK = 128
NB = 18
ROWS = 16
BUCKETS = (12, 13, 14, 18)
VMEM_LIMIT = 61900000


def nn(a, b):
    return jnp.dot(a, b, preferred_element_type=F32)


def nt(a, b):
    return lax.dot_general(a, b, (((1,), (1,)), ((), ())), preferred_element_type=F32)


def iota(shape, dim):
    return lax.broadcasted_iota(jnp.int32, shape, dim)


def flag(cond):
    return jnp.where(cond, 1.0, 0.0).astype(BF)


def act_kernel(
    tok_h, ids_ref, gat_ref, cot_h, wg_h, wu_h, wd_h, msk_ref,
    x_out, y_out, acts, rm, rr, wt, tbl_h, pick_ref,
    tok, cot, wg, wu, wd, sel, wsel, xs, xsr, ys, ysr, xr, xrr, yr, yrr,
    rem, g, u, mx, cells, tbl, cbuf, crec,
    lsem, osem, ssem, rsem,
):
    dp = lax.axis_index("dp")
    me = lax.axis_index("expert")

    loads = [
        pltpu.make_async_copy(tok_h, tok, lsem.at[0]),
        pltpu.make_async_copy(cot_h, cot, lsem.at[1]),
        pltpu.make_async_copy(wg_h, wg, lsem.at[2]),
        pltpu.make_async_copy(wu_h, wu, lsem.at[3]),
        pltpu.make_async_copy(wd_h, wd, lsem.at[4]),
    ]
    for load in loads:
        load.start()

    barrier = pltpu.get_barrier_semaphore()
    for k in range(1, E):
        pl.semaphore_signal(
            barrier, inc=1, device_id=(dp, lax.rem(me + k, E)), device_id_type=MESH
        )

    ids_t = ids_ref[...]
    gat_t = gat_ref[...].astype(BF).astype(F32)
    sub = iota((E, T), 0)
    hit = jnp.zeros((E, T), F32)
    gw = jnp.zeros((E, T), F32)
    for e in range(E):
        same = ids_t == e
        hit = jnp.where(
            sub == e, jnp.sum(jnp.where(same, 1.0, 0.0), axis=0, keepdims=True), hit
        )
        gw = jnp.where(
            sub == e, jnp.sum(jnp.where(same, gat_t, 0.0), axis=0, keepdims=True), gw
        )
    t0 = iota((T, T), 0)
    t1 = iota((T, T), 1)
    earlier = flag((t0 < t1) & ((t0 < TM) == (t1 < TM)))
    before = nn(hit.astype(BF), earlier)
    lane = iota((E, T), 1)
    kept = (hit > 0.0) & (before < float(CAP))
    slot = jnp.where(kept, before + jnp.where(lane < TM, 0.0, float(CAP)), -1.0)
    row8 = iota((T, E), 0)
    owner = jnp.where(row8 < 256, row8 // 32, (row8 - 256) // 4)
    spread = flag(owner == iota((T, E), 1))
    slot_rows = nn(spread, slot.astype(BF))
    want = jnp.where(t0 < 256, t0 % 32, 32 + (t0 - 256) % 4).astype(F32)
    chosen = slot_rows == want
    sel[...] = flag(chosen)

    def dispatch(matrix, source, main, tail):
        for n in range(2):
            cols = slice(1024 * n, 1024 * n + 1024)
            v = nn(matrix[...], source[:, cols])
            main[:, cols] = v[:256].astype(BF)
            for e in range(E):
                tail[e, :, cols] = v[256 + 4 * e : 260 + 4 * e].astype(BF)

    def moves(main, tail, main_to, tail_to, kind):
        out = []
        for k in range(1, E):
            to = lax.rem(me + k, E)
            out.append(
                pltpu.make_async_remote_copy(
                    src_ref=main.at[pl.ds(pl.multiple_of(to * 32, 32), 32)],
                    dst_ref=main_to.at[pl.ds(pl.multiple_of(me * 32, 32), 32)],
                    send_sem=ssem.at[kind, k],
                    recv_sem=rsem.at[kind, k],
                    device_id=(dp, to),
                    device_id_type=MESH,
                )
            )
            out.append(
                pltpu.make_async_remote_copy(
                    src_ref=tail.at[to],
                    dst_ref=tail_to.at[me],
                    send_sem=ssem.at[kind + 1, k],
                    recv_sem=rsem.at[kind + 1, k],
                    device_id=(dp, to),
                    device_id_type=MESH,
                )
            )
        own = [
            pltpu.make_async_copy(
                main.at[pl.ds(pl.multiple_of(me * 32, 32), 32)],
                main_to.at[pl.ds(pl.multiple_of(me * 32, 32), 32)],
                lsem.at[5 + kind],
            ),
            pltpu.make_async_copy(tail.at[me], tail_to.at[me], lsem.at[6 + kind]),
        ]
        return out, own

    def merge(main_to, tail_to):
        for e in range(E):
            rem[4 * e : 4 * e + 4, :] = tail_to[e].astype(F32)
        main_to[256:288, :] = rem[...].astype(BF)

    loads[0].wait()
    dispatch(sel, tok, xs, xsr)
    pl.semaphore_wait(barrier, E - 1)
    x_moves, x_own = moves(xs, xsr, xr, xrr, 0)
    for move in x_moves + x_own:
        move.start()
    gw_rows = nn(spread, gw.astype(BF))
    wsel[...] = jnp.where(chosen, gw_rows, 0.0).astype(BF)
    loads[1].wait()
    dispatch(wsel, cot, ys, ysr)
    y_moves, y_own = moves(ys, ysr, yr, yrr, 2)
    for move in y_moves + y_own:
        move.start()

    widths = (ROWS, BLK)
    for i in range(NB):
        cells[i : i + 1, :] = msk_ref[i].astype(F32)
    place = flag(iota((NB, BLK), 0) == iota((NB, BLK), 1))
    m2 = lax.dot_general(
        cells[0:NB, :].astype(BF), place, (((0,), (0,)), ((), ())), preferred_element_type=F32
    )
    tri = flag(iota((BLK, BLK), 0) <= iota((BLK, BLK), 1))
    upto = nn(m2.astype(BF), tri)
    pos = upto - 1.0
    most = jnp.max(jnp.max(upto, axis=1, keepdims=True), axis=0, keepdims=True)
    cbuf[...] = jnp.broadcast_to(most, (8, BLK))
    order = jnp.zeros(widths, F32)
    cell = iota(widths, 1).astype(F32)
    for i in range(NB):
        here = (pos[:, i : i + 1] == cell) & (m2[:, i : i + 1] > 0.0)
        order = order + jnp.where(here, float(i), 0.0)
    tbl[0:16, :] = order.astype(jnp.int32)
    tbl[16:32, :] = jnp.maximum(pos, 0.0).astype(jnp.int32)
    tbl[32:48, :] = m2.astype(jnp.int32)
    c_moves = []
    for k in range(1, E):
        to = lax.rem(me + k, E)
        c_moves.append(
            pltpu.make_async_remote_copy(
                src_ref=cbuf,
                dst_ref=crec.at[k],
                send_sem=ssem.at[4, k],
                recv_sem=rsem.at[4, k],
                device_id=(dp, to),
                device_id_type=MESH,
            )
        )
    for move in c_moves:
        move.start()

    for mat in range(3):
        lift = flag(iota((BLK, FF), 1) // BLK + 6 * mat == iota((BLK, FF), 0))
        mx[16 * mat : 16 * mat + 16, :] = nn(m2.astype(BF), lift)
    for load in loads[2:]:
        load.wait()

    def prune(r, carry):
        rows = pl.ds(pl.multiple_of(r * BLK, BLK), BLK)
        for mat, w in enumerate((wg, wu, wd)):
            w[rows, :] = w[rows, :] * mx[pl.ds(16 * mat + r, 1), :].astype(BF)
        return carry

    lax.fori_loop(0, ROWS, prune, 0)
    eye = flag(iota((T, T), 0) == iota((T, T), 1))
    wt[...] = nt(eye, wsel[...]).astype(BF)

    put = pltpu.make_async_copy(tbl, tbl_h, osem)
    put.start()

    for move in x_own:
        move.wait()
    for move in x_moves:
        move.wait_recv()
    merge(xr, xrr)
    for n in range(3):
        cols = slice(256 * n, 256 * n + 256)
        gv = nn(xr[...], wg[:, cols])
        uv = nn(xr[...], wu[:, cols])
        g[:, cols] = gv
        u[:, cols] = uv
        h_cols = slice(2 * FF + 256 * n, 2 * FF + 256 * n + 256)
        acts[:, h_cols] = (gv * jax.nn.sigmoid(gv) * uv).astype(BF)
    for n in range(8):
        cols = slice(256 * n, 256 * n + 256)
        v = nt(acts[:, 2 * FF : 3 * FF], wd[cols, :])
        rm[:, cols] = v[:256].astype(BF)
        for e in range(E):
            rr[e, :, cols] = v[256 + 4 * e : 260 + 4 * e].astype(BF)
    x_out[...] = xr[...]

    for move in c_moves:
        move.wait_recv()
    top = cbuf[...]
    for k in range(1, E):
        top = jnp.maximum(top, crec[k])
    peak = top[0, 0]
    pick = jnp.int32(0)
    for cz in BUCKETS[:-1]:
        pick = pick + jnp.where(peak > float(cz), 1, 0).astype(jnp.int32)
    pick_ref[0] = pick

    for move in y_own:
        move.wait()
    for move in y_moves:
        move.wait_recv()
    merge(yr, yrr)
    for n in range(3):
        cols = slice(256 * n, 256 * n + 256)
        u_cols = slice(FF + 256 * n, FF + 256 * n + 256)
        dh = nn(yr[...], wd[:, cols])
        gv = g[:, cols]
        s = jax.nn.sigmoid(gv)
        ds = dh * s
        acts[:, cols] = (ds * u[:, cols] * (1.0 + gv * (1.0 - s))).astype(BF)
        acts[:, u_cols] = (ds * gv).astype(BF)
    y_out[...] = yr[...]
    for move in x_moves + y_moves + c_moves:
        move.wait_send()
    put.wait()


def grad_kernel(
    cz,
    x_ref, y_ref, acts, rm, rr, wt, tbl_h,
    com_h, g_ref,
    tbl, ret, rer, rem, com, blk,
    cs, cr, sm, ra, rb, fp, fm, zz, za, zb, gp, gm,
    lsem, ssem, rsem, csem, crsem, xsem, xrsem, zsem, zrsem,
):
    na = cz // 2
    nb = cz - na
    dp = lax.axis_index("dp")
    me = lax.axis_index("expert")
    x = dp // 8
    z = (dp // 2) % 4
    c = dp % 2

    def at(xx, zz_, cc):
        return ((xx * 4 + zz_) * 2 + cc, me)

    twin = at(x, z, 1 - c)
    xp = at((x + 1) % 4, z, c)
    xm = at((x + 3) % 4, z, c)
    zp = at(x, (z + 1) % 4, c)
    zm = at(x, (z + 3) % 4, c)

    def x_of(i):
        return (x + (2, 1, 3, 0)[i]) % 4

    def z_of(q):
        step = jnp.where(q == 0, 2, jnp.where(q == 1, 1, jnp.where(q == 2, 3, 0)))
        return (z + step) % 4

    barrier = pltpu.get_barrier_semaphore()
    for peer in (twin, xp, xm, zp, zm):
        pl.semaphore_signal(barrier, inc=1, device_id=peer, device_id_type=MESH)
    for k in range(1, E):
        pl.semaphore_signal(
            barrier, inc=1, device_id=(dp, lax.rem(me + k, E)), device_id_type=MESH
        )

    loads = [
        pltpu.make_async_copy(
            rm.at[pl.ds(pl.multiple_of(me * 32, 32), 32)],
            ret.at[pl.ds(pl.multiple_of(me * 32, 32), 32)],
            lsem.at[2],
        ),
        pltpu.make_async_copy(rr.at[me], rer.at[me], lsem.at[3]),
    ]
    tables = pltpu.make_async_copy(tbl_h, tbl, lsem.at[5])
    tables.start()

    r_moves = []
    for k in range(1, E):
        to = lax.rem(me + k, E)
        r_moves.append(
            pltpu.make_async_remote_copy(
                src_ref=rm.at[pl.ds(pl.multiple_of(to * 32, 32), 32)],
                dst_ref=ret.at[pl.ds(pl.multiple_of(me * 32, 32), 32)],
                send_sem=ssem.at[0, k],
                recv_sem=rsem.at[0, k],
                device_id=(dp, to),
                device_id_type=MESH,
            )
        )
        r_moves.append(
            pltpu.make_async_remote_copy(
                src_ref=rr.at[to],
                dst_ref=rer.at[me],
                send_sem=ssem.at[1, k],
                recv_sem=rsem.at[1, k],
                device_id=(dp, to),
                device_id_type=MESH,
            )
        )
    def core_move(t, i):
        s = t * 4 + i
        return pltpu.make_async_remote_copy(
            src_ref=cs.at[s], dst_ref=cr.at[s],
            send_sem=csem.at[s], recv_sem=crsem.at[s],
            device_id=twin, device_id_type=MESH,
        )

    def x_move(kind, t):
        src, dst, peer = (
            lambda: (sm.at[4 * t, pl.ds(0, na)], ra.at[t], xp),
            lambda: (sm.at[4 * t, pl.ds(na, nb)], rb.at[t], xm),
            lambda: (sm.at[4 * t + 1, pl.ds(na, nb)], fp.at[t, pl.ds(na, nb)], xp),
            lambda: (sm.at[4 * t + 2, pl.ds(0, na)], fm.at[t, pl.ds(0, na)], xm),
            lambda: (sm.at[4 * t + 1, pl.ds(0, na)], fp.at[t, pl.ds(0, na)], xp),
            lambda: (sm.at[4 * t + 2, pl.ds(na, nb)], fm.at[t, pl.ds(na, nb)], xm),
        )[kind]()
        return pltpu.make_async_remote_copy(
            src_ref=src, dst_ref=dst,
            send_sem=xsem.at[kind, t], recv_sem=xrsem.at[kind, t],
            device_id=peer, device_id_type=MESH,
        )

    def z_move(kind):
        src, dst, peer = (
            lambda: (zz.at[0, pl.ds(0, na)], za, zp),
            lambda: (zz.at[0, pl.ds(na, nb)], zb, zm),
            lambda: (zz.at[1, pl.ds(na, nb)], gp.at[pl.ds(na, nb)], zp),
            lambda: (zz.at[1, pl.ds(0, na)], gm.at[pl.ds(0, na)], zm),
            lambda: (zz.at[2, pl.ds(0, na)], gp.at[pl.ds(0, na)], zp),
            lambda: (zz.at[2, pl.ds(na, nb)], gm.at[pl.ds(na, nb)], zm),
        )[kind]()
        return pltpu.make_async_remote_copy(
            src_ref=src, dst_ref=dst,
            send_sem=zsem.at[kind], recv_sem=zrsem.at[kind],
            device_id=peer, device_id_type=MESH,
        )

    for load in loads:
        load.start()
    tables.wait()

    def wide(v):
        return v.astype(F32)

    def product(q, carry):
        cols = []
        for i in range(4):
            r = x_of(i) * 4 + z_of(q)
            cols.append(pl.ds(pl.multiple_of(r * BLK, BLK), BLK))
        for n in range(9):
            source = x_ref if n < 6 else y_ref
            v = lax.dot_general(
                jnp.concatenate([source[:, col] for col in cols], axis=1),
                acts[:, 256 * n : 256 * n + 256],
                (((0,), (0,)), ((), ())),
                preferred_element_type=F32,
            )
            for i in range(4):
                for h in range(2):
                    blk[q, i, 2 * n + h] = v[
                        BLK * i : BLK * i + BLK, BLK * h : BLK * h + BLK
                    ].astype(BF)
        return carry

    def round_trip(v, carry):
        lo = jnp.where(v == 0, 0, jnp.where(v == 1, 1, jnp.where(v == 2, 3, 4)))
        hi = jnp.where(v == 0, 1, jnp.where(v == 1, 3, 4))
        lax.fori_loop(lo, hi, product, 0)

        @pl.when(v == 0)
        def _():
            pl.semaphore_wait(barrier, 12)
            for move in r_moves:
                move.start()

        @pl.when(v < 4)
        def _():
            t = v
            q_lo = jnp.where(t == 1, 2, jnp.where(t == 2, 1, t))
            for i in range(4):
                s = 4 * t + i
                for j in range(cz):
                    q = q_lo if j < na else t
                    b = tbl[x_of(i) * 4 + z_of(q), j]
                    cs[s, j] = blk[q, i, b, pl.ds(pl.multiple_of(64 * (1 - c), 64), 64), :]
                    sm[s, j] = blk[q, i, b, pl.ds(pl.multiple_of(64 * c, 64), 64), :]
                core_move(t, i).start()

        @pl.when(v >= 2)
        def _():
            p = v - 2
            for kind in (2, 3, 4, 5):
                x_move(kind, p).wait_recv()
            for j in range(cz):
                zz[p, j] = (
                    wide(sm[4 * p + 3, j]) + wide(fp[p, j]) + wide(fm[p, j])
                ).astype(BF)

        @pl.when(v == 2)
        def _():
            z_move(0).start()
            z_move(1).start()

        @pl.when(v == 3)
        def _():
            z_move(2).start()
            z_move(3).start()

        @pl.when(v == 4)
        def _():
            z_move(0).wait_recv()
            for j in range(na):
                zz[2, j] = (wide(zz[2, j]) + wide(za[j])).astype(BF)
            z_move(4).start()
            z_move(1).wait_recv()
            for j in range(nb):
                zz[2, na + j] = (wide(zz[2, na + j]) + wide(zb[j])).astype(BF)
            z_move(5).start()

        @pl.when(v >= 1)
        def _():
            p = v - 1
            x_move(0, p).wait_recv()
            for j in range(na):
                sm[4 * p + 1, j] = (wide(sm[4 * p + 1, j]) + wide(ra[p, j])).astype(BF)
            x_move(4, p).start()
            x_move(1, p).wait_recv()
            for j in range(nb):
                sm[4 * p + 2, na + j] = (
                    wide(sm[4 * p + 2, na + j]) + wide(rb[p, j])
                ).astype(BF)
            x_move(5, p).start()

        @pl.when(v < 4)
        def _():
            t = v
            for i in range(4):
                s = 4 * t + i
                core_move(t, i).wait_recv()
                for j in range(cz):
                    sm[s, j] = (wide(sm[s, j]) + wide(cr[s, j])).astype(BF)
                if i == 0:
                    x_move(0, t).start()
                    x_move(1, t).start()
                if i == 1:
                    x_move(2, t).start()
                if i == 2:
                    x_move(3, t).start()

        return carry

    lax.fori_loop(0, 5, round_trip, 0)

    for load in loads:
        load.wait()
    for move in r_moves:
        move.wait_recv()
    for e in range(E):
        rem[4 * e : 4 * e + 4, :] = rer[e].astype(F32)
    ret[256:288, :] = rem[...].astype(BF)

    for n in range(4):
        cols = slice(512 * n, 512 * n + 512)
        com[:, cols] = nn(wt[...], ret[:, cols]).astype(BF)
    put = pltpu.make_async_copy(com, com_h, lsem.at[4])
    put.start()

    for kind in (2, 3, 4, 5):
        x_move(kind, 3).wait_recv()
        z_move(kind).wait_recv()
    r = x * 4 + z
    for i in range(NB):
        p = tbl[16 + r, i]
        m = tbl[32 + r, i].astype(F32)
        v = wide(sm[15, p]) + wide(fp[3, p]) + wide(fm[3, p]) + wide(gp[p]) + wide(gm[p])
        g_ref[i // 6, :, BLK * (i % 6) : BLK * (i % 6) + BLK] = v * m

    for move in r_moves:
        move.wait_send()

    def drain(t, carry):
        for i in range(4):
            core_move(t, i).wait_send()
        for kind in range(6):
            x_move(kind, t).wait_send()
        return carry

    lax.fori_loop(0, 4, drain, 0)
    for kind in range(6):
        z_move(kind).wait_send()
    put.wait()


def final_kernel(com_h, g_h, out_h, gg_h, gu_h, gd_h, com, grad, isem, osem):
    loads = [
        pltpu.make_async_copy(
            com_h.at[pl.ds(96 * k, 96)], com.at[pl.ds(96 * k, 96)], isem.at[k]
        )
        for k in range(3)
    ] + [pltpu.make_async_copy(g_h.at[k], grad.at[k], isem.at[3 + k]) for k in range(3)]
    puts = [
        pltpu.make_async_copy(
            com.at[pl.ds(96 * k, 96)], out_h.at[pl.ds(96 * k, 96)], osem.at[k]
        )
        for k in range(3)
    ] + [
        pltpu.make_async_copy(grad.at[k], (gg_h, gu_h, gd_h)[k], osem.at[3 + k])
        for k in range(3)
    ]
    for load in loads:
        load.start()
    for load, put in zip(loads, puts):
        load.wait()
        put.start()
    for put in puts:
        put.wait()


def body(tokens, expert_ids, gates, cotangent, gate_weight, up_weight, down_weight, block_masks):
    any_spec = pl.BlockSpec(memory_space=pltpu.HBM)
    vmem = pl.BlockSpec(memory_space=pltpu.VMEM)
    shape = jax.ShapeDtypeStruct
    dma = pltpu.SemaphoreType.DMA
    smem = pl.BlockSpec(memory_space=pltpu.SMEM)
    x, y, acts, rm, rr, wt, tbl, pick = pl.pallas_call(
        act_kernel,
        out_shape=[
            shape((T, D), BF),
            shape((T, D), BF),
            shape((T, 3 * FF), BF),
            shape((256, D), BF),
            shape((E, 4, D), BF),
            shape((T, T), BF),
            shape((48, BLK), jnp.int32),
            shape((1,), jnp.int32),
        ],
        in_specs=[any_spec, vmem, vmem] + [any_spec] * 4 + [vmem],
        out_specs=[vmem] * 6 + [any_spec, smem],
        scratch_shapes=[
            pltpu.VMEM((T, D), BF),
            pltpu.VMEM((T, D), BF),
            pltpu.VMEM((D, FF), BF),
            pltpu.VMEM((D, FF), BF),
            pltpu.VMEM((D, FF), BF),
            pltpu.VMEM((T, T), BF),
            pltpu.VMEM((T, T), BF),
            pltpu.VMEM((256, D), BF),
            pltpu.VMEM((E, 4, D), BF),
            pltpu.VMEM((256, D), BF),
            pltpu.VMEM((E, 4, D), BF),
            pltpu.VMEM((T, D), BF),
            pltpu.VMEM((E, 4, D), BF),
            pltpu.VMEM((T, D), BF),
            pltpu.VMEM((E, 4, D), BF),
            pltpu.VMEM((32, D), F32),
            pltpu.VMEM((T, FF), F32),
            pltpu.VMEM((T, FF), F32),
            pltpu.VMEM((48, FF), F32),
            pltpu.VMEM((24, ROWS), F32),
            pltpu.VMEM((48, BLK), jnp.int32),
            pltpu.VMEM((8, BLK), F32),
            pltpu.VMEM((E, 8, BLK), F32),
            dma((9,)),
            dma(()),
            dma((5, E)),
            dma((5, E)),
        ],
        compiler_params=pltpu.CompilerParams(
            collective_id=0, has_side_effects=True, vmem_limit_bytes=VMEM_LIMIT
        ),
        name="act",
    )(
        tokens, expert_ids.T, gates.T, cotangent,
        gate_weight[0], up_weight[0], down_weight[0],
        block_masks.transpose(1, 3, 0, 2).reshape(NB, 1, ROWS),
    )

    def grads(index, cz):
        na, nb = cz // 2, cz - cz // 2

        def buf(*lead):
            return pltpu.VMEM(lead + (64, BLK), BF)

        return pl.pallas_call(
            functools.partial(grad_kernel, cz),
            out_shape=[
                shape((T, D), BF),
                shape((3, 64, FF), F32),
            ],
            in_specs=[vmem] * 6 + [any_spec],
            out_specs=[any_spec, vmem],
            scratch_shapes=[
                pltpu.SMEM((48, BLK), jnp.int32),
                pltpu.VMEM((T, D), BF),
                pltpu.VMEM((E, 4, D), BF),
                pltpu.VMEM((32, D), F32),
                pltpu.VMEM((T, D), BF),
                pltpu.VMEM((4, 4, NB, BLK, BLK), BF),
                buf(16, cz), buf(16, cz), buf(16, cz),
                buf(4, na), buf(4, nb), buf(4, cz), buf(4, cz),
                buf(3, cz), buf(na), buf(nb), buf(cz), buf(cz),
                dma((6,)),
                dma((2, E)),
                dma((2, E)),
                dma((16,)),
                dma((16,)),
                dma((6, 4)),
                dma((6, 4)),
                dma((6,)),
                dma((6,)),
            ],
            compiler_params=pltpu.CompilerParams(
                collective_id=1 + index, has_side_effects=True, vmem_limit_bytes=VMEM_LIMIT
            ),
            name=f"grad{cz}",
        )

    combined, g3 = lax.switch(
        pick[0],
        [lambda *ops, f=grads(i, cz): tuple(f(*ops)) for i, cz in enumerate(BUCKETS)],
        x, y, acts, rm, rr, wt, tbl,
    )
    combined, gg, gu, gd = pl.pallas_call(
        final_kernel,
        out_shape=[shape((T, D), BF)] + [shape((64, FF), F32)] * 3,
        in_specs=[any_spec] * 2,
        out_specs=[any_spec] * 4,
        scratch_shapes=[
            pltpu.VMEM((T, D), BF),
            pltpu.VMEM((3, 64, FF), F32),
            dma((6,)),
            dma((6,)),
        ],
        name="final",
    )(combined, g3)
    return (combined, gg[None], gu[None], gd[None])


def solution(mesh):
    return jax.shard_map(
        body,
        mesh=mesh,
        in_specs=(
            P(("dp", "expert"), None),
            P(("dp", "expert"), None),
            P(("dp", "expert"), None),
            P(("dp", "expert"), None),
            P("expert", None, None),
            P("expert", None, None),
            P("expert", None, None),
            P("expert", None, None, None),
        ),
        out_specs=(
            P(("dp", "expert"), None),
            P("expert", "dp", None),
            P("expert", "dp", None),
            P("expert", "dp", None),
        ),
        check_vma=False,
    )
```

```python
import functools

import jax
import jax.numpy as jnp
from jax import lax
from jax.experimental import pallas as pl
from jax.experimental.pallas import tpu as pltpu
from jax.sharding import PartitionSpec as P

MESH = pl.DeviceIdType.MESH
BF = jnp.bfloat16
F32 = jnp.float32
CAP = 18
E = 8
T = 288
TM = 144
D = 2048
FF = 768
BLK = 128
NB = 18
ROWS = 16
BUCKETS = ((13, 9, 18), (14, 11, 20), (16, 14, 24), (18, 24, 42))
HEAD = 6
VMEM_LIMIT = 61900000


def nn(a, b):
    return jnp.dot(a, b, preferred_element_type=F32)


def nt(a, b):
    return lax.dot_general(a, b, (((1,), (1,)), ((), ())), preferred_element_type=F32)


def iota(shape, dim):
    return lax.broadcasted_iota(jnp.int32, shape, dim)


def flag(cond):
    return jnp.where(cond, 1.0, 0.0).astype(BF)


def act_kernel(
    tok_h, ids_ref, gat_ref, cot_h, wg_h, wu_h, wd_h, msk_ref,
    x_out, y_out, acts, rm, rr, wt, tbl_h, pick_ref,
    tok, cot, wg, wu, wd, sel, wsel, xs, xsr, ys, ysr, xr, xrr, yr, yrr,
    rem, g, u, mx, cells, tbl, cbuf, crec,
    lsem, osem, ssem, rsem,
):
    dp = lax.axis_index("dp")
    me = lax.axis_index("expert")

    loads = [
        pltpu.make_async_copy(tok_h, tok, lsem.at[0]),
        pltpu.make_async_copy(cot_h, cot, lsem.at[1]),
        pltpu.make_async_copy(wg_h, wg, lsem.at[2]),
        pltpu.make_async_copy(wu_h, wu, lsem.at[3]),
        pltpu.make_async_copy(wd_h, wd, lsem.at[4]),
    ]
    for load in loads:
        load.start()

    barrier = pltpu.get_barrier_semaphore()
    for k in range(1, E):
        pl.semaphore_signal(
            barrier, inc=1, device_id=(dp, lax.rem(me + k, E)), device_id_type=MESH
        )

    ids_t = ids_ref[...]
    gat_t = gat_ref[...].astype(BF).astype(F32)
    sub = iota((E, T), 0)
    hit = jnp.zeros((E, T), F32)
    gw = jnp.zeros((E, T), F32)
    for e in range(E):
        same = ids_t == e
        hit = jnp.where(
            sub == e, jnp.sum(jnp.where(same, 1.0, 0.0), axis=0, keepdims=True), hit
        )
        gw = jnp.where(
            sub == e, jnp.sum(jnp.where(same, gat_t, 0.0), axis=0, keepdims=True), gw
        )
    t0 = iota((T, T), 0)
    t1 = iota((T, T), 1)
    earlier = flag((t0 < t1) & ((t0 < TM) == (t1 < TM)))
    before = nn(hit.astype(BF), earlier)
    lane = iota((E, T), 1)
    kept = (hit > 0.0) & (before < float(CAP))
    slot = jnp.where(kept, before + jnp.where(lane < TM, 0.0, float(CAP)), -1.0)
    row8 = iota((T, E), 0)
    owner = jnp.where(row8 < 256, row8 // 32, (row8 - 256) // 4)
    spread = flag(owner == iota((T, E), 1))
    slot_rows = nn(spread, slot.astype(BF))
    want = jnp.where(t0 < 256, t0 % 32, 32 + (t0 - 256) % 4).astype(F32)
    chosen = slot_rows == want
    sel[...] = flag(chosen)

    def dispatch(matrix, source, main, tail):
        for n in range(2):
            cols = slice(1024 * n, 1024 * n + 1024)
            v = nn(matrix[...], source[:, cols])
            main[:, cols] = v[:256].astype(BF)
            for e in range(E):
                tail[e, :, cols] = v[256 + 4 * e : 260 + 4 * e].astype(BF)

    def moves(main, tail, main_to, tail_to, kind):
        out = []
        for k in range(1, E):
            to = lax.rem(me + k, E)
            out.append(
                pltpu.make_async_remote_copy(
                    src_ref=main.at[pl.ds(pl.multiple_of(to * 32, 32), 32)],
                    dst_ref=main_to.at[pl.ds(pl.multiple_of(me * 32, 32), 32)],
                    send_sem=ssem.at[kind, k],
                    recv_sem=rsem.at[kind, k],
                    device_id=(dp, to),
                    device_id_type=MESH,
                )
            )
            out.append(
                pltpu.make_async_remote_copy(
                    src_ref=tail.at[to],
                    dst_ref=tail_to.at[me],
                    send_sem=ssem.at[kind + 1, k],
                    recv_sem=rsem.at[kind + 1, k],
                    device_id=(dp, to),
                    device_id_type=MESH,
                )
            )
        own = [
            pltpu.make_async_copy(
                main.at[pl.ds(pl.multiple_of(me * 32, 32), 32)],
                main_to.at[pl.ds(pl.multiple_of(me * 32, 32), 32)],
                lsem.at[5 + kind],
            ),
            pltpu.make_async_copy(tail.at[me], tail_to.at[me], lsem.at[6 + kind]),
        ]
        return out, own

    def merge(main_to, tail_to):
        for e in range(E):
            rem[4 * e : 4 * e + 4, :] = tail_to[e].astype(F32)
        main_to[256:288, :] = rem[...].astype(BF)

    loads[0].wait()
    dispatch(sel, tok, xs, xsr)
    pl.semaphore_wait(barrier, E - 1)
    x_moves, x_own = moves(xs, xsr, xr, xrr, 0)
    for move in x_moves + x_own:
        move.start()
    gw_rows = nn(spread, gw.astype(BF))
    wsel[...] = jnp.where(chosen, gw_rows, 0.0).astype(BF)
    loads[1].wait()
    dispatch(wsel, cot, ys, ysr)
    y_moves, y_own = moves(ys, ysr, yr, yrr, 2)
    for move in y_moves + y_own:
        move.start()

    widths = (ROWS, BLK)
    for i in range(NB):
        cells[i : i + 1, :] = msk_ref[i].astype(F32)
    place = flag(iota((NB, BLK), 0) == iota((NB, BLK), 1))
    m2 = lax.dot_general(
        cells[0:NB, :].astype(BF), place, (((0,), (0,)), ((), ())), preferred_element_type=F32
    )
    tri = flag(iota((BLK, BLK), 0) <= iota((BLK, BLK), 1))
    upto = nn(m2.astype(BF), tri)
    pos = upto - 1.0
    order = jnp.zeros(widths, F32)
    cell = iota(widths, 1).astype(F32)
    for i in range(NB):
        here = (pos[:, i : i + 1] == cell) & (m2[:, i : i + 1] > 0.0)
        order = order + jnp.where(here, float(i), 0.0)
    r_i = iota((ROWS, ROWS), 0)
    r_j = iota((ROWS, ROWS), 1)
    line = r_i // 4 == r_j // 4
    before_z = flag(line & (r_j % 4 == (r_i + 3) % 4))
    after_z = flag(line & (r_j % 4 == (r_i + 1) % 4))
    count = jnp.broadcast_to(upto[:, BLK - 1 :], widths)
    o_prev = nn(before_z, order.astype(BF))
    o_next = nn(after_z, order.astype(BF))
    c_prev = nn(before_z, count.astype(BF))
    c_next = nn(after_z, count.astype(BF))
    rest_prev = jnp.maximum(c_prev - float(HEAD), 0.0)
    rest = rest_prev + jnp.maximum(c_next - float(HEAD), 0.0)
    shift = flag(iota((BLK, BLK), 1) == iota((BLK, BLK), 0) + HEAD)
    heads = jnp.where(
        cell < float(HEAD),
        o_prev + 36.0,
        jnp.where(cell < float(2 * HEAD), nn(o_next.astype(BF), shift) + 18.0, 0.0),
    )
    tails = jnp.zeros(widths, F32)
    for i in range(NB):
        here = (cell == rest + float(i)) & (count > float(i))
        tails = tails + jnp.where(here, order[:, i : i + 1] + 54.0, 0.0)
    for i in range(HEAD, NB):
        here = (cell == float(i - HEAD)) & (c_prev > float(i))
        tails = tails + jnp.where(here, o_prev[:, i : i + 1] + 36.0, 0.0)
        here = (cell == rest_prev + float(i - HEAD)) & (c_next > float(i))
        tails = tails + jnp.where(here, o_next[:, i : i + 1] + 18.0, 0.0)
    sizes = jnp.where(cell == 0.0, count, jnp.where(cell == 1.0, rest, rest + count))
    cbuf[...] = jnp.broadcast_to(jnp.max(sizes, axis=0, keepdims=True), (8, BLK))
    tbl[0:16, :] = order.astype(jnp.int32)
    tbl[16:32, :] = heads.astype(jnp.int32)
    tbl[32:48, :] = tails.astype(jnp.int32)
    tbl[48:64, :] = jnp.maximum(pos, 0.0).astype(jnp.int32)
    tbl[64:80, :] = m2.astype(jnp.int32)
    tbl[80:96, :] = count.astype(jnp.int32)
    c_moves = []
    for k in range(1, E):
        to = lax.rem(me + k, E)
        c_moves.append(
            pltpu.make_async_remote_copy(
                src_ref=cbuf,
                dst_ref=crec.at[k],
                send_sem=ssem.at[4, k],
                recv_sem=rsem.at[4, k],
                device_id=(dp, to),
                device_id_type=MESH,
            )
        )
    for move in c_moves:
        move.start()

    for mat in range(3):
        lift = flag(iota((BLK, FF), 1) // BLK + 6 * mat == iota((BLK, FF), 0))
        mx[16 * mat : 16 * mat + 16, :] = nn(m2.astype(BF), lift)
    for load in loads[2:]:
        load.wait()

    def prune(r, carry):
        rows = pl.ds(pl.multiple_of(r * BLK, BLK), BLK)
        for mat, w in enumerate((wg, wu, wd)):
            w[rows, :] = w[rows, :] * mx[pl.ds(16 * mat + r, 1), :].astype(BF)
        return carry

    lax.fori_loop(0, ROWS, prune, 0)
    eye = flag(iota((T, T), 0) == iota((T, T), 1))
    wt[...] = nt(eye, wsel[...]).astype(BF)

    put = pltpu.make_async_copy(tbl, tbl_h, osem)
    put.start()

    for move in x_own:
        move.wait()
    for move in x_moves:
        move.wait_recv()
    merge(xr, xrr)
    for n in range(3):
        cols = slice(256 * n, 256 * n + 256)
        gv = nn(xr[...], wg[:, cols])
        uv = nn(xr[...], wu[:, cols])
        g[:, cols] = gv
        u[:, cols] = uv
        h_cols = slice(2 * FF + 256 * n, 2 * FF + 256 * n + 256)
        acts[:, h_cols] = (gv * jax.nn.sigmoid(gv) * uv).astype(BF)
    for n in range(8):
        cols = slice(256 * n, 256 * n + 256)
        v = nt(acts[:, 2 * FF : 3 * FF], wd[cols, :])
        rm[:, cols] = v[:256].astype(BF)
        for e in range(E):
            rr[e, :, cols] = v[256 + 4 * e : 260 + 4 * e].astype(BF)
    x_out[...] = xr[...]

    for move in c_moves:
        move.wait_recv()
    top = cbuf[...]
    for k in range(1, E):
        top = jnp.maximum(top, crec[k])
    pick = jnp.int32(0)
    for bucket in BUCKETS[:-1]:
        over = top[0, 0] > float(bucket[0])
        for k in (1, 2):
            over = over | (top[0, k] > float(bucket[k]))
        pick = pick + jnp.where(over, 1, 0).astype(jnp.int32)
    pick_ref[0] = pick

    for move in y_own:
        move.wait()
    for move in y_moves:
        move.wait_recv()
    merge(yr, yrr)
    for n in range(3):
        cols = slice(256 * n, 256 * n + 256)
        u_cols = slice(FF + 256 * n, FF + 256 * n + 256)
        dh = nn(yr[...], wd[:, cols])
        gv = g[:, cols]
        s = jax.nn.sigmoid(gv)
        ds = dh * s
        acts[:, cols] = (ds * u[:, cols] * (1.0 + gv * (1.0 - s))).astype(BF)
        acts[:, u_cols] = (ds * gv).astype(BF)
    y_out[...] = yr[...]
    for move in x_moves + y_moves + c_moves:
        move.wait_send()
    put.wait()


def grad_kernel(
    bucket,
    x_ref, y_ref, acts, rm, rr, wt, tbl_h,
    com_h, g_ref,
    tbl, ret, rer, rem, com, blk,
    cs, cr, sm, ra, rb, fp, fm, zz, za, zb, gp, gm, zt, zu, fin,
    lsem, ssem, rsem, csem, crsem, xsem, xrsem, zsem, zrsem,
):
    cz, k2, total = bucket
    ks = (cz, 2 * HEAD, k2, total - k2)
    km = max(ks)
    tail = cz - HEAD
    dp = lax.axis_index("dp")
    me = lax.axis_index("expert")
    x = dp // 8
    z = (dp // 2) % 4
    c = dp % 2

    def at(xx, zz_, cc):
        return ((xx * 4 + zz_) * 2 + cc, me)

    twin = at(x, z, 1 - c)
    xp = at((x + 1) % 4, z, c)
    xm = at((x + 3) % 4, z, c)
    zp = at(x, (z + 1) % 4, c)
    zm = at(x, (z + 3) % 4, c)

    def x_of(i):
        return (x + (2, 1, 3, 0)[i]) % 4

    def z_of(q):
        step = jnp.where(q == 0, 2, jnp.where(q == 1, 1, jnp.where(q == 2, 3, 0)))
        return (z + step) % 4

    barrier = pltpu.get_barrier_semaphore()
    for peer in (twin, xp, xm, zp, zm):
        pl.semaphore_signal(barrier, inc=1, device_id=peer, device_id_type=MESH)
    for k in range(1, E):
        pl.semaphore_signal(
            barrier, inc=1, device_id=(dp, lax.rem(me + k, E)), device_id_type=MESH
        )

    loads = [
        pltpu.make_async_copy(
            rm.at[pl.ds(pl.multiple_of(me * 32, 32), 32)],
            ret.at[pl.ds(pl.multiple_of(me * 32, 32), 32)],
            lsem.at[2],
        ),
        pltpu.make_async_copy(rr.at[me], rer.at[me], lsem.at[3]),
    ]
    tables = pltpu.make_async_copy(tbl_h, tbl, lsem.at[5])
    tables.start()

    r_moves = []
    for k in range(1, E):
        to = lax.rem(me + k, E)
        r_moves.append(
            pltpu.make_async_remote_copy(
                src_ref=rm.at[pl.ds(pl.multiple_of(to * 32, 32), 32)],
                dst_ref=ret.at[pl.ds(pl.multiple_of(me * 32, 32), 32)],
                send_sem=ssem.at[0, k],
                recv_sem=rsem.at[0, k],
                device_id=(dp, to),
                device_id_type=MESH,
            )
        )
        r_moves.append(
            pltpu.make_async_remote_copy(
                src_ref=rr.at[to],
                dst_ref=rer.at[me],
                send_sem=ssem.at[1, k],
                recv_sem=rsem.at[1, k],
                device_id=(dp, to),
                device_id_type=MESH,
            )
        )
    def core_move(t, i):
        s = t * 4 + i
        return pltpu.make_async_remote_copy(
            src_ref=cs.at[s], dst_ref=cr.at[s],
            send_sem=csem.at[s], recv_sem=crsem.at[s],
            device_id=twin, device_id_type=MESH,
        )

    def x_move(kind, t):
        low, high = pl.ds(0, HEAD), pl.ds(HEAD, ks[t] - HEAD)
        src, dst, peer = (
            lambda: (sm.at[4 * t, low], ra.at[t], xp),
            lambda: (sm.at[4 * t, high], rb.at[t, pl.ds(0, ks[t] - HEAD)], xm),
            lambda: (sm.at[4 * t + 1, high], fp.at[t, high], xp),
            lambda: (sm.at[4 * t + 2, low], fm.at[t, low], xm),
            lambda: (sm.at[4 * t + 1, low], fp.at[t, low], xp),
            lambda: (sm.at[4 * t + 2, high], fm.at[t, high], xm),
        )[kind]()
        return pltpu.make_async_remote_copy(
            src_ref=src, dst_ref=dst,
            send_sem=xsem.at[kind, t], recv_sem=xrsem.at[kind, t],
            device_id=peer, device_id_type=MESH,
        )

    def z_move(kind):
        src, dst, peer = (
            lambda: (zz.at[0, pl.ds(0, HEAD)], za, zp),
            lambda: (zz.at[0, pl.ds(HEAD, tail)], zb, zm),
            lambda: (zz.at[1, pl.ds(0, HEAD)], gm.at[pl.ds(0, HEAD)], zm),
            lambda: (zz.at[1, pl.ds(HEAD, HEAD)], gp.at[pl.ds(0, HEAD)], zp),
            lambda: (zt, gp.at[pl.ds(HEAD, tail)], zp),
            lambda: (zu, gm.at[pl.ds(HEAD, tail)], zm),
        )[kind]()
        return pltpu.make_async_remote_copy(
            src_ref=src, dst_ref=dst,
            send_sem=zsem.at[kind], recv_sem=zrsem.at[kind],
            device_id=peer, device_id_type=MESH,
        )

    for load in loads:
        load.start()
    tables.wait()

    def wide(v):
        return v.astype(F32)

    def product(q, carry):
        cols = []
        for i in range(4):
            r = x_of(i) * 4 + z_of(q)
            cols.append(pl.ds(pl.multiple_of(r * BLK, BLK), BLK))
        for n in range(9):
            source = x_ref if n < 6 else y_ref
            v = lax.dot_general(
                jnp.concatenate([source[:, col] for col in cols], axis=1),
                acts[:, 256 * n : 256 * n + 256],
                (((0,), (0,)), ((), ())),
                preferred_element_type=F32,
            )
            for i in range(4):
                for h in range(2):
                    blk[i, q * NB + 2 * n + h] = v[
                        BLK * i : BLK * i + BLK, BLK * h : BLK * h + BLK
                    ].astype(BF)
        return carry

    def per_round(v, lag, action, rounds=4):
        for t in range(rounds):

            @pl.when(v == t + lag)
            def _(t=t):
                action(t)

    def size_of(t):
        return jnp.where(
            t == 0, ks[0], jnp.where(t == 1, ks[1], jnp.where(t == 2, ks[2], ks[3]))
        )

    rest = [
        jnp.maximum(tbl[80 + 4 * x + (z + step) % 4, 0] - HEAD, 0) for step in (3, 1)
    ]

    def round_trip(v, carry):
        lo = jnp.where(v == 0, 0, jnp.where(v == 1, 1, jnp.where(v == 2, 3, 4)))
        hi = jnp.where(v == 0, 1, jnp.where(v == 1, 3, 4))
        lax.fori_loop(lo, hi, product, 0)

        @pl.when(v == 0)
        def _():
            pl.semaphore_wait(barrier, 12)
            for move in r_moves:
                move.start()

        @pl.when(v < 4)
        def _():
            t = v
            base = jnp.where(t == 0, z_of(0), jnp.where(t == 1, 16 + z, 32 + z))
            off = jnp.where(t == 3, k2, 0)
            for i in range(4):
                s = 4 * t + i
                for j in range(km):
                    b = tbl[x_of(i) * 4 + base, off + j]
                    cs[s, j] = blk[i, b, pl.ds(pl.multiple_of(64 * (1 - c), 64), 64), :]
                    sm[s, j] = blk[i, b, pl.ds(pl.multiple_of(64 * c, 64), 64), :]
                core_move(t, i).start()

        def x_landed(t):
            for kind in (2, 3, 4, 5):
                x_move(kind, t).wait_recv()

        per_round(v, 2, x_landed, 3)

        @pl.when(v >= 2)
        def _():
            p = v - 2

            def add(j):
                zz[p, j] = (
                    wide(sm[4 * p + 3, j]) + wide(fp[p, j]) + wide(fm[p, j])
                ).astype(BF)

            def step(j, carry):
                add(j)
                return carry

            for j in range(HEAD):
                add(j)
            lax.fori_loop(HEAD, size_of(p), step, 0)

        @pl.when(v == 2)
        def _():
            z_move(0).start()
            z_move(1).start()

        @pl.when(v == 3)
        def _():
            z_move(2).start()

        @pl.when(v == 4)
        def _():
            for j in range(tail):
                zt[j] = zz[2, jnp.minimum(rest[0] + j, k2 - 1)]
            z_move(4).start()
            z_move(1).wait_recv()
            for j in range(tail):
                zu[j] = (wide(zz[2, j]) + wide(zb[j])).astype(BF)
            z_move(5).start()

        per_round(v, 1, lambda t: x_move(0, t).wait_recv())

        @pl.when(v >= 1)
        def _():
            p = v - 1
            for j in range(HEAD):
                sm[4 * p + 1, j] = (wide(sm[4 * p + 1, j]) + wide(ra[p, j])).astype(BF)

        def relay(t):
            x_move(4, t).start()
            x_move(1, t).wait_recv()

        per_round(v, 1, relay)

        @pl.when(v >= 1)
        def _():
            p = v - 1

            def step(j, carry):
                sm[4 * p + 2, HEAD + j] = (
                    wide(sm[4 * p + 2, HEAD + j]) + wide(rb[p, j])
                ).astype(BF)
                return carry

            lax.fori_loop(0, size_of(p) - HEAD, step, 0)

        per_round(v, 1, lambda t: x_move(5, t).start())

        for i in range(4):

            @pl.when(v < 4)
            def _(i=i):
                t = v
                s = 4 * t + i
                core_move(t, i).wait_recv()
                for j in range(km):
                    sm[s, j] = (wide(sm[s, j]) + wide(cr[s, j])).astype(BF)

            def send(t, i=i):
                for kind in ((0, 1), (2,), (3,))[i]:
                    x_move(kind, t).start()

            if i < 3:
                per_round(v, 0, send)

        @pl.when(v == 3)
        def _():
            z_move(0).wait_recv()
            for j in range(HEAD):
                zz[1, HEAD + j] = (wide(zz[1, HEAD + j]) + wide(za[j])).astype(BF)
            z_move(3).start()

        return carry

    lax.fori_loop(0, 5, round_trip, 0)

    for load in loads:
        load.wait()
    for move in r_moves:
        move.wait_recv()
    for e in range(E):
        rem[4 * e : 4 * e + 4, :] = rer[e].astype(F32)
    ret[256:288, :] = rem[...].astype(BF)

    for n in range(4):
        cols = slice(512 * n, 512 * n + 512)
        com[:, cols] = nn(wt[...], ret[:, cols]).astype(BF)
    put = pltpu.make_async_copy(com, com_h, lsem.at[4])
    put.start()

    for j in range(k2):
        fin[j] = wide(sm[11, j]) + wide(fp[2, j]) + wide(fm[2, j])
    for kind in (2, 3, 4, 5):
        x_move(kind, 3).wait_recv()
    for j in range(total - k2):
        fin[k2 + j] = wide(sm[15, j]) + wide(fp[3, j]) + wide(fm[3, j])
    for kind in (2, 3, 4, 5):
        z_move(kind).wait_recv()
    r = x * 4 + z
    for i in range(NB):
        p = tbl[48 + r, i]
        m = tbl[64 + r, i].astype(F32)
        f = jnp.minimum(rest[0] + rest[1] + p, total - 1)
        g_ref[i // 6, :, BLK * (i % 6) : BLK * (i % 6) + BLK] = (
            fin[f] + wide(gp[p]) + wide(gm[p])
        ) * m

    for move in r_moves:
        move.wait_send()

    for t in range(4):
        for i in range(4):
            core_move(t, i).wait_send()
        for kind in range(6):
            x_move(kind, t).wait_send()
    for kind in range(6):
        z_move(kind).wait_send()
    put.wait()


def final_kernel(com_h, g_h, out_h, gg_h, gu_h, gd_h, com, grad, isem, osem):
    loads = [
        pltpu.make_async_copy(
            com_h.at[pl.ds(96 * k, 96)], com.at[pl.ds(96 * k, 96)], isem.at[k]
        )
        for k in range(3)
    ] + [pltpu.make_async_copy(g_h.at[k], grad.at[k], isem.at[3 + k]) for k in range(3)]
    puts = [
        pltpu.make_async_copy(
            com.at[pl.ds(96 * k, 96)], out_h.at[pl.ds(96 * k, 96)], osem.at[k]
        )
        for k in range(3)
    ] + [
        pltpu.make_async_copy(grad.at[k], (gg_h, gu_h, gd_h)[k], osem.at[3 + k])
        for k in range(3)
    ]
    for load in loads:
        load.start()
    for load, put in zip(loads, puts):
        load.wait()
        put.start()
    for put in puts:
        put.wait()


def body(tokens, expert_ids, gates, cotangent, gate_weight, up_weight, down_weight, block_masks):
    any_spec = pl.BlockSpec(memory_space=pltpu.HBM)
    vmem = pl.BlockSpec(memory_space=pltpu.VMEM)
    shape = jax.ShapeDtypeStruct
    dma = pltpu.SemaphoreType.DMA
    smem = pl.BlockSpec(memory_space=pltpu.SMEM)
    x, y, acts, rm, rr, wt, tbl, pick = pl.pallas_call(
        act_kernel,
        out_shape=[
            shape((T, D), BF),
            shape((T, D), BF),
            shape((T, 3 * FF), BF),
            shape((256, D), BF),
            shape((E, 4, D), BF),
            shape((T, T), BF),
            shape((96, BLK), jnp.int32),
            shape((1,), jnp.int32),
        ],
        in_specs=[any_spec, vmem, vmem] + [any_spec] * 4 + [vmem],
        out_specs=[vmem] * 6 + [any_spec, smem],
        scratch_shapes=[
            pltpu.VMEM((T, D), BF),
            pltpu.VMEM((T, D), BF),
            pltpu.VMEM((D, FF), BF),
            pltpu.VMEM((D, FF), BF),
            pltpu.VMEM((D, FF), BF),
            pltpu.VMEM((T, T), BF),
            pltpu.VMEM((T, T), BF),
            pltpu.VMEM((256, D), BF),
            pltpu.VMEM((E, 4, D), BF),
            pltpu.VMEM((256, D), BF),
            pltpu.VMEM((E, 4, D), BF),
            pltpu.VMEM((T, D), BF),
            pltpu.VMEM((E, 4, D), BF),
            pltpu.VMEM((T, D), BF),
            pltpu.VMEM((E, 4, D), BF),
            pltpu.VMEM((32, D), F32),
            pltpu.VMEM((T, FF), F32),
            pltpu.VMEM((T, FF), F32),
            pltpu.VMEM((48, FF), F32),
            pltpu.VMEM((24, ROWS), F32),
            pltpu.VMEM((96, BLK), jnp.int32),
            pltpu.VMEM((8, BLK), F32),
            pltpu.VMEM((E, 8, BLK), F32),
            dma((9,)),
            dma(()),
            dma((5, E)),
            dma((5, E)),
        ],
        compiler_params=pltpu.CompilerParams(
            collective_id=0, has_side_effects=True, vmem_limit_bytes=VMEM_LIMIT
        ),
        name="act",
    )(
        tokens, expert_ids.T, gates.T, cotangent,
        gate_weight[0], up_weight[0], down_weight[0],
        block_masks.transpose(1, 3, 0, 2).reshape(NB, 1, ROWS),
    )

    def grads(index, bucket):
        cz, k2, total = bucket
        km = max(cz, 2 * HEAD, k2, total - k2)
        tail = cz - HEAD

        def buf(*lead):
            return pltpu.VMEM(lead + (64, BLK), BF)

        return pl.pallas_call(
            functools.partial(grad_kernel, bucket),
            out_shape=[
                shape((T, D), BF),
                shape((3, 64, FF), F32),
            ],
            in_specs=[vmem] * 6 + [any_spec],
            out_specs=[any_spec, vmem],
            scratch_shapes=[
                pltpu.SMEM((96, BLK), jnp.int32),
                pltpu.VMEM((T, D), BF),
                pltpu.VMEM((E, 4, D), BF),
                pltpu.VMEM((32, D), F32),
                pltpu.VMEM((T, D), BF),
                pltpu.VMEM((4, 4 * NB, BLK, BLK), BF),
                buf(16, km), buf(16, km), buf(16, km),
                buf(4, HEAD), buf(4, km - HEAD), buf(4, km), buf(4, km),
                buf(3, km), buf(HEAD), buf(tail), buf(cz), buf(cz), buf(tail), buf(tail),
                pltpu.VMEM((total, 64, BLK), F32),
                dma((6,)),
                dma((2, E)),
                dma((2, E)),
                dma((16,)),
                dma((16,)),
                dma((6, 4)),
                dma((6, 4)),
                dma((6,)),
                dma((6,)),
            ],
            compiler_params=pltpu.CompilerParams(
                collective_id=1 + index, has_side_effects=True, vmem_limit_bytes=VMEM_LIMIT
            ),
            name=f"grad{index}",
        )

    combined, g3 = lax.switch(
        pick[0],
        [lambda *ops, f=grads(i, b): tuple(f(*ops)) for i, b in enumerate(BUCKETS)],
        x, y, acts, rm, rr, wt, tbl,
    )
    combined, gg, gu, gd = pl.pallas_call(
        final_kernel,
        out_shape=[shape((T, D), BF)] + [shape((64, FF), F32)] * 3,
        in_specs=[any_spec] * 2,
        out_specs=[any_spec] * 4,
        scratch_shapes=[
            pltpu.VMEM((T, D), BF),
            pltpu.VMEM((3, 64, FF), F32),
            dma((6,)),
            dma((6,)),
        ],
        name="final",
    )(combined, g3)
    return (combined, gg[None], gu[None], gd[None])


def solution(mesh):
    return jax.shard_map(
        body,
        mesh=mesh,
        in_specs=(
            P(("dp", "expert"), None),
            P(("dp", "expert"), None),
            P(("dp", "expert"), None),
            P(("dp", "expert"), None),
            P("expert", None, None),
            P("expert", None, None),
            P("expert", None, None),
            P("expert", None, None, None),
        ),
        out_specs=(
            P(("dp", "expert"), None),
            P("expert", "dp", None),
            P("expert", "dp", None),
            P("expert", "dp", None),
        ),
        check_vma=False,
    )
```

```python
import functools

import jax
import jax.numpy as jnp
from jax import lax
from jax.experimental import pallas as pl
from jax.experimental.pallas import tpu as pltpu
from jax.sharding import PartitionSpec as P

MESH = pl.DeviceIdType.MESH
BF = jnp.bfloat16
F32 = jnp.float32
CAP = 18
E = 8
T = 288
TM = 144
D = 2048
FF = 768
BLK = 128
NB = 18
ROWS = 16
BUCKETS = (11, 12, 13, 14, 15, 18)
VMEM_LIMIT = 61900000


def nn(a, b):
    return jnp.dot(a, b, preferred_element_type=F32)


def nt(a, b):
    return lax.dot_general(a, b, (((1,), (1,)), ((), ())), preferred_element_type=F32)


def iota(shape, dim):
    return lax.broadcasted_iota(jnp.int32, shape, dim)


def flag(cond):
    return jnp.where(cond, 1.0, 0.0).astype(BF)


def act_kernel(
    tok_h, ids_ref, gat_ref, cot_h, wg_h, wu_h, wd_h, msk_ref,
    x_out, y_out, acts, rm, rr, wt, tbl_h, pick_ref,
    tok, cot, wg, wu, wd, sel, wsel, xs, xsr, ys, ysr, xr, xrr, yr, yrr,
    rem, g, u, mx, cells, tbl, cbuf, crec,
    lsem, osem, ssem, rsem,
):
    dp = lax.axis_index("dp")
    me = lax.axis_index("expert")

    loads = [
        pltpu.make_async_copy(tok_h, tok, lsem.at[0]),
        pltpu.make_async_copy(cot_h, cot, lsem.at[1]),
        pltpu.make_async_copy(wg_h, wg, lsem.at[2]),
        pltpu.make_async_copy(wu_h, wu, lsem.at[3]),
        pltpu.make_async_copy(wd_h, wd, lsem.at[4]),
    ]
    for load in loads:
        load.start()

    barrier = pltpu.get_barrier_semaphore()
    for k in range(1, E):
        pl.semaphore_signal(
            barrier, inc=1, device_id=(dp, lax.rem(me + k, E)), device_id_type=MESH
        )

    ids_t = ids_ref[...]
    gat_t = gat_ref[...].astype(BF).astype(F32)
    sub = iota((E, T), 0)
    hit = jnp.zeros((E, T), F32)
    for e in range(E):
        same = ids_t == e
        hit = jnp.where(
            sub == e, jnp.sum(jnp.where(same, 1.0, 0.0), axis=0, keepdims=True), hit
        )
    t0 = iota((T, T), 0)
    t1 = iota((T, T), 1)
    earlier = flag((t0 < t1) & ((t0 < TM) == (t1 < TM)))
    before = nn(hit.astype(BF), earlier)
    lane = iota((E, T), 1)
    kept = (hit > 0.0) & (before < float(CAP))
    slot = jnp.where(kept, before + jnp.where(lane < TM, 0.0, float(CAP)), -1.0)
    row8 = iota((T, E), 0)
    owner = jnp.where(row8 < 256, row8 // 32, (row8 - 256) // 4)
    spread = flag(owner == iota((T, E), 1))
    slot_rows = nn(spread, slot.astype(BF))
    want = jnp.where(t0 < 256, t0 % 32, 32 + (t0 - 256) % 4).astype(F32)
    chosen = slot_rows == want
    sel[...] = flag(chosen)

    def dispatch(matrix, source, main, tail):
        for n in range(2):
            cols = slice(1024 * n, 1024 * n + 1024)
            v = nn(matrix[...], source[:, cols])
            main[:, cols] = v[:256].astype(BF)
            for e in range(E):
                tail[e, :, cols] = v[256 + 4 * e : 260 + 4 * e].astype(BF)

    def moves(main, tail, main_to, tail_to, kind):
        out = []
        for k in range(1, E):
            to = lax.rem(me + k, E)
            out.append(
                pltpu.make_async_remote_copy(
                    src_ref=main.at[pl.ds(pl.multiple_of(to * 32, 32), 32)],
                    dst_ref=main_to.at[pl.ds(pl.multiple_of(me * 32, 32), 32)],
                    send_sem=ssem.at[kind, k],
                    recv_sem=rsem.at[kind, k],
                    device_id=(dp, to),
                    device_id_type=MESH,
                )
            )
            out.append(
                pltpu.make_async_remote_copy(
                    src_ref=tail.at[to],
                    dst_ref=tail_to.at[me],
                    send_sem=ssem.at[kind + 1, k],
                    recv_sem=rsem.at[kind + 1, k],
                    device_id=(dp, to),
                    device_id_type=MESH,
                )
            )
        own = [
            pltpu.make_async_copy(
                main.at[pl.ds(pl.multiple_of(me * 32, 32), 32)],
                main_to.at[pl.ds(pl.multiple_of(me * 32, 32), 32)],
                lsem.at[5 + kind],
            ),
            pltpu.make_async_copy(tail.at[me], tail_to.at[me], lsem.at[6 + kind]),
        ]
        return out, own

    def merge(main_to, tail_to):
        for e in range(E):
            rem[4 * e : 4 * e + 4, :] = tail_to[e].astype(F32)
        main_to[256:288, :] = rem[...].astype(BF)

    loads[0].wait()
    dispatch(sel, tok, xs, xsr)
    pl.semaphore_wait(barrier, E - 1)
    x_moves, x_own = moves(xs, xsr, xr, xrr, 0)
    for move in x_moves + x_own:
        move.start()
    gw = jnp.zeros((E, T), F32)
    for e in range(E):
        gw = jnp.where(
            sub == e, jnp.sum(jnp.where(ids_t == e, gat_t, 0.0), axis=0, keepdims=True), gw
        )
    gw_rows = nn(spread, gw.astype(BF))
    wsel[...] = jnp.where(chosen, gw_rows, 0.0).astype(BF)
    loads[1].wait()
    dispatch(wsel, cot, ys, ysr)
    y_moves, y_own = moves(ys, ysr, yr, yrr, 2)
    for move in y_moves + y_own:
        move.start()

    widths = (ROWS, BLK)
    for i in range(NB):
        cells[i : i + 1, :] = msk_ref[i].astype(F32)
    place = flag(iota((NB, BLK), 0) == iota((NB, BLK), 1))
    m2 = lax.dot_general(
        cells[0:NB, :].astype(BF), place, (((0,), (0,)), ((), ())), preferred_element_type=F32
    )
    tri = flag(iota((BLK, BLK), 0) <= iota((BLK, BLK), 1))
    upto = nn(m2.astype(BF), tri)
    pos = upto - 1.0
    most = jnp.max(jnp.max(upto, axis=1, keepdims=True), axis=0, keepdims=True)
    cbuf[...] = jnp.broadcast_to(most, (8, BLK))
    order = jnp.zeros(widths, F32)
    cell = iota(widths, 1).astype(F32)
    for i in range(NB):
        here = (pos[:, i : i + 1] == cell) & (m2[:, i : i + 1] > 0.0)
        order = order + jnp.where(here, float(i), 0.0)
    tbl[0:16, :] = order.astype(jnp.int32)
    tbl[16:32, :] = jnp.maximum(pos, 0.0).astype(jnp.int32)
    tbl[32:48, :] = m2.astype(jnp.int32)
    c_moves = []
    for k in range(1, E):
        to = lax.rem(me + k, E)
        c_moves.append(
            pltpu.make_async_remote_copy(
                src_ref=cbuf,
                dst_ref=crec.at[k],
                send_sem=ssem.at[4, k],
                recv_sem=rsem.at[4, k],
                device_id=(dp, to),
                device_id_type=MESH,
            )
        )
    for move in c_moves:
        move.start()

    for mat in range(3):
        lift = flag(iota((BLK, FF), 1) // BLK + 6 * mat == iota((BLK, FF), 0))
        mx[16 * mat : 16 * mat + 16, :] = nn(m2.astype(BF), lift)
    for load in loads[2:]:
        load.wait()

    def prune(r, carry):
        rows = pl.ds(pl.multiple_of(r * BLK, BLK), BLK)
        for mat, w in enumerate((wg, wu, wd)):
            w[rows, :] = w[rows, :] * mx[pl.ds(16 * mat + r, 1), :].astype(BF)
        return carry

    lax.fori_loop(0, ROWS, prune, 0)
    eye = flag(iota((T, T), 0) == iota((T, T), 1))
    wt[...] = nt(eye, wsel[...]).astype(BF)

    put = pltpu.make_async_copy(tbl, tbl_h, osem)
    put.start()

    for move in x_own:
        move.wait()
    for move in x_moves:
        move.wait_recv()
    merge(xr, xrr)
    for n in range(3):
        cols = slice(256 * n, 256 * n + 256)
        gv = nn(xr[...], wg[:, cols])
        uv = nn(xr[...], wu[:, cols])
        g[:, cols] = gv
        u[:, cols] = uv
        h_cols = slice(2 * FF + 256 * n, 2 * FF + 256 * n + 256)
        acts[:, h_cols] = (gv * jax.nn.sigmoid(gv) * uv).astype(BF)
    for n in range(8):
        cols = slice(256 * n, 256 * n + 256)
        v = nt(acts[:, 2 * FF : 3 * FF], wd[cols, :])
        rm[:, cols] = v[:256].astype(BF)
        for e in range(E):
            rr[e, :, cols] = v[256 + 4 * e : 260 + 4 * e].astype(BF)
    x_out[...] = xr[...]

    for move in c_moves:
        move.wait_recv()
    top = cbuf[...]
    for k in range(1, E):
        top = jnp.maximum(top, crec[k])
    peak = top[0, 0]
    pick = jnp.int32(0)
    for cz in BUCKETS[:-1]:
        pick = pick + jnp.where(peak > float(cz), 1, 0).astype(jnp.int32)
    pick_ref[0] = pick

    for move in y_own:
        move.wait()
    for move in y_moves:
        move.wait_recv()
    merge(yr, yrr)
    for n in range(3):
        cols = slice(256 * n, 256 * n + 256)
        u_cols = slice(FF + 256 * n, FF + 256 * n + 256)
        dh = nn(yr[...], wd[:, cols])
        gv = g[:, cols]
        s = jax.nn.sigmoid(gv)
        ds = dh * s
        acts[:, cols] = (ds * u[:, cols] * (1.0 + gv * (1.0 - s))).astype(BF)
        acts[:, u_cols] = (ds * gv).astype(BF)
    y_out[...] = yr[...]
    for move in x_moves + y_moves + c_moves:
        move.wait_send()
    put.wait()


def grad_kernel(
    cz,
    x_ref, y_ref, acts, rm, rr, wt, tbl_h,
    com_h, g_h,
    tbl, ret, rer, rem, com, grad, blk,
    cs, cr, sm, ra, rb, fp, fm, zz, za, zb, gp, gm,
    gsem, lsem, ssem, rsem, csem, crsem, xsem, xrsem, zsem, zrsem,
):
    na = cz // 2
    nb = cz - na
    dp = lax.axis_index("dp")
    me = lax.axis_index("expert")
    x = dp // 8
    z = (dp // 2) % 4
    c = dp % 2

    def at(xx, zz_, cc):
        return ((xx * 4 + zz_) * 2 + cc, me)

    twin = at(x, z, 1 - c)
    xp = at((x + 1) % 4, z, c)
    xm = at((x + 3) % 4, z, c)
    zp = at(x, (z + 1) % 4, c)
    zm = at(x, (z + 3) % 4, c)

    def x_of(i):
        return (x + (2, 1, 3, 0)[i]) % 4

    def z_of(q):
        step = jnp.where(q == 0, 2, jnp.where(q == 1, 1, jnp.where(q == 2, 3, 0)))
        return (z + step) % 4

    barrier = pltpu.get_barrier_semaphore()
    for peer in (twin, xp, xm, zp, zm):
        pl.semaphore_signal(barrier, inc=1, device_id=peer, device_id_type=MESH)
    for k in range(1, E):
        pl.semaphore_signal(
            barrier, inc=1, device_id=(dp, lax.rem(me + k, E)), device_id_type=MESH
        )

    loads = [
        pltpu.make_async_copy(
            rm.at[pl.ds(pl.multiple_of(me * 32, 32), 32)],
            ret.at[pl.ds(pl.multiple_of(me * 32, 32), 32)],
            lsem.at[2],
        ),
        pltpu.make_async_copy(rr.at[me], rer.at[me], lsem.at[3]),
    ]
    tables = pltpu.make_async_copy(tbl_h, tbl, lsem.at[5])
    tables.start()

    r_moves = []
    for k in range(1, E):
        to = lax.rem(me + k, E)
        r_moves.append(
            pltpu.make_async_remote_copy(
                src_ref=rm.at[pl.ds(pl.multiple_of(to * 32, 32), 32)],
                dst_ref=ret.at[pl.ds(pl.multiple_of(me * 32, 32), 32)],
                send_sem=ssem.at[0, k],
                recv_sem=rsem.at[0, k],
                device_id=(dp, to),
                device_id_type=MESH,
            )
        )
        r_moves.append(
            pltpu.make_async_remote_copy(
                src_ref=rr.at[to],
                dst_ref=rer.at[me],
                send_sem=ssem.at[1, k],
                recv_sem=rsem.at[1, k],
                device_id=(dp, to),
                device_id_type=MESH,
            )
        )
    def core_move(t, i):
        s = t * 4 + i
        return pltpu.make_async_remote_copy(
            src_ref=cs.at[s], dst_ref=cr.at[s],
            send_sem=csem.at[s], recv_sem=crsem.at[s],
            device_id=twin, device_id_type=MESH,
        )

    def x_move(kind, t):
        src, dst, peer = (
            lambda: (sm.at[4 * t, pl.ds(0, na)], ra.at[t], xp),
            lambda: (sm.at[4 * t, pl.ds(na, nb)], rb.at[t], xm),
            lambda: (sm.at[4 * t + 1, pl.ds(na, nb)], fp.at[t, pl.ds(na, nb)], xp),
            lambda: (sm.at[4 * t + 2, pl.ds(0, na)], fm.at[t, pl.ds(0, na)], xm),
            lambda: (sm.at[4 * t + 1, pl.ds(0, na)], fp.at[t, pl.ds(0, na)], xp),
            lambda: (sm.at[4 * t + 2, pl.ds(na, nb)], fm.at[t, pl.ds(na, nb)], xm),
        )[kind]()
        return pltpu.make_async_remote_copy(
            src_ref=src, dst_ref=dst,
            send_sem=xsem.at[kind, t], recv_sem=xrsem.at[kind, t],
            device_id=peer, device_id_type=MESH,
        )

    def z_move(kind):
        src, dst, peer = (
            lambda: (zz.at[0, pl.ds(0, na)], za, zp),
            lambda: (zz.at[0, pl.ds(na, nb)], zb, zm),
            lambda: (zz.at[1, pl.ds(na, nb)], gp.at[pl.ds(na, nb)], zp),
            lambda: (zz.at[1, pl.ds(0, na)], gm.at[pl.ds(0, na)], zm),
            lambda: (zz.at[2, pl.ds(0, na)], gp.at[pl.ds(0, na)], zp),
            lambda: (zz.at[2, pl.ds(na, nb)], gm.at[pl.ds(na, nb)], zm),
        )[kind]()
        return pltpu.make_async_remote_copy(
            src_ref=src, dst_ref=dst,
            send_sem=zsem.at[kind], recv_sem=zrsem.at[kind],
            device_id=peer, device_id_type=MESH,
        )

    for load in loads:
        load.start()
    tables.wait()

    def wide(v):
        return v.astype(F32)

    def product(q, carry):
        cols = []
        for i in range(4):
            r = x_of(i) * 4 + z_of(q)
            cols.append(pl.ds(pl.multiple_of(r * BLK, BLK), BLK))
        for n in range(9):
            source = x_ref if n < 6 else y_ref
            v = lax.dot_general(
                jnp.concatenate([source[:, col] for col in cols], axis=1),
                acts[:, 256 * n : 256 * n + 256],
                (((0,), (0,)), ((), ())),
                preferred_element_type=F32,
            )
            for i in range(4):
                for h in range(2):
                    blk[q, i, 2 * n + h] = v[
                        BLK * i : BLK * i + BLK, BLK * h : BLK * h + BLK
                    ].astype(BF)
        return carry

    def round_trip(v, carry):
        lo = jnp.where(v == 0, 0, jnp.where(v == 1, 1, jnp.where(v == 2, 3, 4)))
        hi = jnp.where(v == 0, 1, jnp.where(v == 1, 3, 4))
        lax.fori_loop(lo, hi, product, 0)

        @pl.when(v == 0)
        def _():
            pl.semaphore_wait(barrier, 12)

        @pl.when(v < 4)
        def _():
            t = v
            q_lo = jnp.where(t == 1, 2, jnp.where(t == 2, 1, t))
            for i in range(4):
                s = 4 * t + i
                for j in range(cz):
                    q = q_lo if j < na else t
                    b = tbl[x_of(i) * 4 + z_of(q), j]
                    cs[s, j] = blk[q, i, b, pl.ds(pl.multiple_of(64 * (1 - c), 64), 64), :]
                    sm[s, j] = blk[q, i, b, pl.ds(pl.multiple_of(64 * c, 64), 64), :]
                core_move(t, i).start()

        @pl.when(v == 0)
        def _():
            for move in r_moves:
                move.start()

        @pl.when(v >= 2)
        def _():
            p = v - 2
            for kind in (2, 3, 4, 5):
                x_move(kind, p).wait_recv()
            for j in range(cz):
                zz[p, j] = (
                    wide(sm[4 * p + 3, j]) + wide(fp[p, j]) + wide(fm[p, j])
                ).astype(BF)

        @pl.when(v == 2)
        def _():
            z_move(0).start()
            z_move(1).start()

        @pl.when(v == 3)
        def _():
            z_move(2).start()
            z_move(3).start()

        @pl.when(v == 4)
        def _():
            z_move(0).wait_recv()
            for j in range(na):
                zz[2, j] = (wide(zz[2, j]) + wide(za[j])).astype(BF)
            z_move(4).start()
            z_move(1).wait_recv()
            for j in range(nb):
                zz[2, na + j] = (wide(zz[2, na + j]) + wide(zb[j])).astype(BF)
            z_move(5).start()

        @pl.when(v >= 1)
        def _():
            p = v - 1
            x_move(0, p).wait_recv()
            for j in range(na):
                sm[4 * p + 1, j] = (wide(sm[4 * p + 1, j]) + wide(ra[p, j])).astype(BF)
            x_move(4, p).start()
            x_move(1, p).wait_recv()
            for j in range(nb):
                sm[4 * p + 2, na + j] = (
                    wide(sm[4 * p + 2, na + j]) + wide(rb[p, j])
                ).astype(BF)
            x_move(5, p).start()

        @pl.when(v < 4)
        def _():
            t = v
            for i in range(4):
                s = 4 * t + i
                core_move(t, i).wait_recv()
                for j in range(cz):
                    sm[s, j] = (wide(sm[s, j]) + wide(cr[s, j])).astype(BF)
                if i == 0:
                    x_move(0, t).start()
                    x_move(1, t).start()
                if i == 1:
                    x_move(2, t).start()
                if i == 2:
                    x_move(3, t).start()

        return carry

    lax.fori_loop(0, 5, round_trip, 0)

    for load in loads:
        load.wait()
    for move in r_moves:
        move.wait_recv()
    for e in range(E):
        rem[4 * e : 4 * e + 4, :] = rer[e].astype(F32)
    ret[256:288, :] = rem[...].astype(BF)

    for n in range(4):
        cols = slice(512 * n, 512 * n + 512)
        com[:, cols] = nn(wt[...], ret[:, cols]).astype(BF)
    put = pltpu.make_async_copy(com, com_h, lsem.at[4])
    put.start()

    for kind in (2, 3, 4, 5):
        x_move(kind, 3).wait_recv()
        z_move(kind).wait_recv()
    def leave(k):
        return pltpu.make_async_copy(grad.at[k], g_h.at[k], gsem.at[k])

    r = x * 4 + z
    for i in range(NB):
        p = tbl[16 + r, i]
        m = tbl[32 + r, i].astype(F32)
        v = wide(sm[15, p]) + wide(fp[3, p]) + wide(fm[3, p]) + wide(gp[p]) + wide(gm[p])
        grad[i // 6, :, BLK * (i % 6) : BLK * (i % 6) + BLK] = v * m
        if i % 6 == 5:
            leave(i // 6).start()

    for move in r_moves:
        move.wait_send()

    def drain(t, carry):
        for i in range(4):
            core_move(t, i).wait_send()
        for kind in range(6):
            x_move(kind, t).wait_send()
        return carry

    lax.fori_loop(0, 4, drain, 0)
    for kind in range(6):
        z_move(kind).wait_send()
    put.wait()
    for k in range(3):
        leave(k).wait()


def final_kernel(com_h, g_h, out_h, gg_h, gu_h, gd_h, com, grad, isem, osem):
    loads = [
        pltpu.make_async_copy(
            com_h.at[pl.ds(96 * k, 96)], com.at[pl.ds(96 * k, 96)], isem.at[k]
        )
        for k in range(3)
    ] + [pltpu.make_async_copy(g_h.at[k], grad.at[k], isem.at[3 + k]) for k in range(3)]
    puts = [
        pltpu.make_async_copy(
            com.at[pl.ds(96 * k, 96)], out_h.at[pl.ds(96 * k, 96)], osem.at[k]
        )
        for k in range(3)
    ] + [
        pltpu.make_async_copy(grad.at[k], (gg_h, gu_h, gd_h)[k], osem.at[3 + k])
        for k in range(3)
    ]
    for load in loads:
        load.start()
    for load, put in zip(loads, puts):
        load.wait()
        put.start()
    for put in puts:
        put.wait()


def body(tokens, expert_ids, gates, cotangent, gate_weight, up_weight, down_weight, block_masks):
    any_spec = pl.BlockSpec(memory_space=pltpu.HBM)
    vmem = pl.BlockSpec(memory_space=pltpu.VMEM)
    shape = jax.ShapeDtypeStruct
    dma = pltpu.SemaphoreType.DMA
    smem = pl.BlockSpec(memory_space=pltpu.SMEM)
    x, y, acts, rm, rr, wt, tbl, pick = pl.pallas_call(
        act_kernel,
        out_shape=[
            shape((T, D), BF),
            shape((T, D), BF),
            shape((T, 3 * FF), BF),
            shape((256, D), BF),
            shape((E, 4, D), BF),
            shape((T, T), BF),
            shape((48, BLK), jnp.int32),
            shape((1,), jnp.int32),
        ],
        in_specs=[any_spec, vmem, vmem] + [any_spec] * 4 + [vmem],
        out_specs=[vmem] * 6 + [any_spec, smem],
        scratch_shapes=[
            pltpu.VMEM((T, D), BF),
            pltpu.VMEM((T, D), BF),
            pltpu.VMEM((D, FF), BF),
            pltpu.VMEM((D, FF), BF),
            pltpu.VMEM((D, FF), BF),
            pltpu.VMEM((T, T), BF),
            pltpu.VMEM((T, T), BF),
            pltpu.VMEM((256, D), BF),
            pltpu.VMEM((E, 4, D), BF),
            pltpu.VMEM((256, D), BF),
            pltpu.VMEM((E, 4, D), BF),
            pltpu.VMEM((T, D), BF),
            pltpu.VMEM((E, 4, D), BF),
            pltpu.VMEM((T, D), BF),
            pltpu.VMEM((E, 4, D), BF),
            pltpu.VMEM((32, D), F32),
            pltpu.VMEM((T, FF), F32),
            pltpu.VMEM((T, FF), F32),
            pltpu.VMEM((48, FF), F32),
            pltpu.VMEM((24, ROWS), F32),
            pltpu.VMEM((48, BLK), jnp.int32),
            pltpu.VMEM((8, BLK), F32),
            pltpu.VMEM((E, 8, BLK), F32),
            dma((9,)),
            dma(()),
            dma((5, E)),
            dma((5, E)),
        ],
        compiler_params=pltpu.CompilerParams(
            collective_id=0, has_side_effects=True, vmem_limit_bytes=VMEM_LIMIT
        ),
        name="act",
    )(
        tokens, expert_ids.T, gates.T, cotangent,
        gate_weight[0], up_weight[0], down_weight[0],
        block_masks.transpose(1, 3, 0, 2).reshape(NB, 1, ROWS),
    )

    def grads(index, cz):
        na, nb = cz // 2, cz - cz // 2

        def buf(*lead):
            return pltpu.VMEM(lead + (64, BLK), BF)

        return pl.pallas_call(
            functools.partial(grad_kernel, cz),
            out_shape=[
                shape((T, D), BF),
                shape((3, 64, FF), F32),
            ],
            in_specs=[vmem] * 6 + [any_spec],
            out_specs=[any_spec, any_spec],
            scratch_shapes=[
                pltpu.SMEM((48, BLK), jnp.int32),
                pltpu.VMEM((T, D), BF),
                pltpu.VMEM((E, 4, D), BF),
                pltpu.VMEM((32, D), F32),
                pltpu.VMEM((T, D), BF),
                pltpu.VMEM((3, 64, FF), F32),
                pltpu.VMEM((4, 4, NB, BLK, BLK), BF),
                buf(16, cz), buf(16, cz), buf(16, cz),
                buf(4, na), buf(4, nb), buf(4, cz), buf(4, cz),
                buf(3, cz), buf(na), buf(nb), buf(cz), buf(cz),
                dma((3,)),
                dma((6,)),
                dma((2, E)),
                dma((2, E)),
                dma((16,)),
                dma((16,)),
                dma((6, 4)),
                dma((6, 4)),
                dma((6,)),
                dma((6,)),
            ],
            compiler_params=pltpu.CompilerParams(
                collective_id=1 + index, has_side_effects=True, vmem_limit_bytes=VMEM_LIMIT
            ),
            name=f"grad{cz}",
        )

    combined, g3 = lax.switch(
        pick[0],
        [lambda *ops, f=grads(i, cz): tuple(f(*ops)) for i, cz in enumerate(BUCKETS)],
        x, y, acts, rm, rr, wt, tbl,
    )
    combined, gg, gu, gd = pl.pallas_call(
        final_kernel,
        out_shape=[shape((T, D), BF)] + [shape((64, FF), F32)] * 3,
        in_specs=[any_spec] * 2,
        out_specs=[any_spec] * 4,
        scratch_shapes=[
            pltpu.VMEM((T, D), BF),
            pltpu.VMEM((3, 64, FF), F32),
            dma((6,)),
            dma((6,)),
        ],
        name="final",
    )(combined, g3)
    return (combined, gg[None], gu[None], gd[None])


def solution(mesh):
    return jax.shard_map(
        body,
        mesh=mesh,
        in_specs=(
            P(("dp", "expert"), None),
            P(("dp", "expert"), None),
            P(("dp", "expert"), None),
            P(("dp", "expert"), None),
            P("expert", None, None),
            P("expert", None, None),
            P("expert", None, None),
            P("expert", None, None, None),
        ),
        out_specs=(
            P(("dp", "expert"), None),
            P("expert", "dp", None),
            P("expert", "dp", None),
            P("expert", "dp", None),
        ),
        check_vma=False,
    )
```
